32 devices in a mesh: groups: 2 (over x), tok: 16 (over z, y, core).
Axes of the slice: x: 2, y: 2, z: 4, core: 2. Of those that a mesh axis runs over, the one named last changes fastest.
Arguments:
- query_tokens: bfloat16 [3, 4096, 1024], P(None, ('groups', 'tok')), parts along dimension 1, may hold values from -6 to 6
- key_tokens: bfloat16 [3, 4096, 1024], P(None, ('groups', 'tok')), parts along dimension 1, may hold values from -6 to 6
- value_tokens: bfloat16 [3, 4096, 1024], P(None, ('groups', 'tok')), parts along dimension 1, may hold values from -6 to 6
- learn_rates: float32 [3, 4096, 2], P(None, ('groups', 'tok')), parts along dimension 1, may hold values from 0.0009765625 to 0.00390625
- fast_first: bfloat16 [2, 512, 512], P(None, 'tok'), may hold values from -0.25 to 0.25
- fast_third: bfloat16 [2, 512, 512], P(None, 'tok'), may hold values from -0.25 to 0.25
- fast_second: bfloat16 [2, 512, 512], P(None, 'tok'), may hold values from -0.25 to 0.25
- momentum_decay: float32 [2], replicated, may hold values from 0.3 to 0.95
Outputs:
- readout: bfloat16 [3, 4096, 1024], P(None, ('groups', 'tok')), parts along dimension 1
The draws below stay inside these ranges and needn't reach their ends.
There are 2 independent parts, one for each index of `groups`. The reference program is written for one: setup_inputs(seed, part) draws one part's arguments, and reference() takes and returns one part's arrays. A program takes and returns all parts, laid end to end along the dimension named above; an argument that names none is the same for every part. Nothing has to cross between parts.
All inputs are finite; a program needn't handle non-finite values.
Results may differ from the reference program's by a relative error of at most 0.0089.
Values may be sent and summed in bfloat16 or wider, within the bound.
A program may use at most 64 MiB of HBM per device.

```python
import math
import jax
import jax.numpy as jnp
from jax import lax

HEADS = 2
HD = 512
FH = 512
NCHUNK = 3
TOK_DEV = 128
CH = 2048


def raised(array, key, source, target, parts, factor):
    owner, partner = [(jnp.arange(array.shape[axis_at]) // (array.shape[axis_at] // parts)).reshape([-1 if axis == axis_at else 1 for axis in range(array.ndim)]) for axis_at in (source, target)]
    chosen = jax.random.permutation(key, parts)[partner]
    strong = (owner == chosen) | (owner == (partner + parts // 2) % parts)
    return jnp.where(strong, factor * array, array)


def block_scale(key, dims, cuts, least, largest):
    gain = 1.0
    for dim, parts in cuts:
        steps = jax.random.uniform(jax.random.fold_in(jax.random.fold_in(key, 6), dim), (parts,), jnp.float32, least / len(cuts), largest / len(cuts))
        gain = gain * jnp.repeat(jnp.exp(steps), dims[dim] // parts).reshape((-1,) + (1,) * (len(dims) - 1 - dim))
    return gain


def centred(stream_key, extent, scale, most, cuts=(), kind=jnp.bfloat16):
    values = jax.random.normal(stream_key, extent, jnp.float32) * scale
    if len(cuts) > 0:
        values = block_scale(stream_key, extent, cuts, -0.22, 0.18) * values
    return jnp.clip(values, min=-most, max=most).astype(kind)


def bell_draw_with(key, shape, spread, reach, shards, heavy, kind=jnp.bfloat16):
    values = spread * jax.random.normal(key, shape, jnp.float32)
    if shards:
        values = values * block_scale(key, shape, shards, -0.22, 0.18)
    return jnp.clip(raised(values, jax.random.fold_in(key, 3), *heavy), -reach, reach).astype(kind)


def setup_inputs(seed: int = 0, part: int = 0) -> dict:
    seeds = jax.random.split(jax.random.key(seed), 9)
    own_keys = jax.random.split(jax.random.fold_in(seeds[8], part), 9)
    return {
        "query_tokens": centred(own_keys[0], (NCHUNK, CH, HEADS * HD), 1.0, 6.0, ((1, 16),)),
        "key_tokens": centred(own_keys[1], (NCHUNK, CH, HEADS * HD), 1.0, 6.0, ((1, 16),)),
        "value_tokens": bell_draw_with(own_keys[2], (NCHUNK, CH, HEADS * HD), 1.0, 6.0, ((1, 16),), (1, 2, 16, 2.0)),
        "learn_rates": jnp.clip(jnp.exp(math.log(0.00390625) - 1.3862944 * jax.random.uniform(own_keys[3], (NCHUNK, CH, HEADS), jnp.float32) ** block_scale(own_keys[3], (NCHUNK, CH, HEADS), ((1, 16),), -0.2, 0.2)), 0.0009765625, 0.00390625),
        "fast_first": centred(seeds[4], (HEADS, FH, HD), HD ** -0.5, 0.25, ((1, 16),)),
        "fast_third": centred(seeds[5], (HEADS, FH, HD), HD ** -0.5, 0.25, ((1, 16),)),
        "fast_second": centred(seeds[6], (HEADS, HD, FH), FH ** -0.5, 0.25, ((1, 16),)),
        "momentum_decay": jnp.clip(jax.random.uniform(seeds[7], (HEADS,), jnp.float32, 0.3, 0.95), 0.3, 0.95),
    }


def forward_parts(weights, inputs):
    first, third, second = weights
    length = inputs.shape[0]
    head_count = first.shape[0]
    shaped = inputs.reshape(length, head_count, -1).astype(jnp.float32)
    pre_gate = jnp.einsum('thd,hfd->htf', shaped, first.astype(jnp.float32))
    pre_up = jnp.einsum('thd,hfd->htf', shaped, third.astype(jnp.float32))
    hidden = (jax.nn.silu(pre_gate) * pre_up).astype(jnp.bfloat16)
    return (shaped, pre_gate, pre_up, hidden)

def apply_block(weights, inputs):
    shaped, pre_gate, pre_up, hidden = forward_parts(weights, inputs)
    result = jnp.einsum('htf,hdf->thd', hidden.astype(jnp.float32), weights[2].astype(jnp.float32))
    return result.reshape(inputs.shape[0], -1)

def apply_all(weights, inputs):
    blocks = inputs.reshape(CH // TOK_DEV, TOK_DEV, inputs.shape[1])
    result = lax.map(lambda piece: apply_block(weights, piece), blocks)
    return result.reshape(CH, inputs.shape[1])

def step_block(weights, keys, values, rates):
    shaped, pre_gate, pre_up, hidden = forward_parts(weights, keys)
    length = keys.shape[0]
    head_count = weights[0].shape[0]
    scaled = (rates[:, :, None] * values.reshape(length, head_count, -1).astype(jnp.float32)).astype(jnp.bfloat16).astype(jnp.float32)
    step_second = jnp.einsum('thd,htf->hdf', scaled, hidden.astype(jnp.float32))
    back = jnp.einsum('thd,hdf->htf', scaled, weights[2].astype(jnp.float32))
    sig_gate = jax.nn.sigmoid(pre_gate)
    d_gate = (back * pre_up * sig_gate * (1.0 + pre_gate * (1.0 - sig_gate))).astype(jnp.bfloat16).astype(jnp.float32)
    d_up = (back * pre_gate * sig_gate).astype(jnp.bfloat16).astype(jnp.float32)
    step_first = jnp.einsum('htf,thd->hfd', d_gate, shaped)
    step_third = jnp.einsum('htf,thd->hfd', d_up, shaped)
    return (step_first, step_third, step_second)

def step_all(weights, keys, values, rates):
    width = keys.shape[1]
    key_blocks = keys.reshape(CH // TOK_DEV, TOK_DEV, width)
    value_blocks = values.reshape(CH // TOK_DEV, TOK_DEV, width)
    rate_blocks = rates.reshape(CH // TOK_DEV, TOK_DEV, rates.shape[1])
    start = tuple((jnp.zeros(w.shape, jnp.float32) for w in weights))

    def advance(carry, pieces):
        terms = step_block(weights, pieces[0], pieces[1], pieces[2])
        return (tuple((c + s for c, s in zip(carry, terms))), None)
    total, unused = lax.scan(advance, start, (key_blocks, value_blocks, rate_blocks))
    return total

def renorm(old, moved):
    old_norm = jnp.sqrt(lax.optimization_barrier(jnp.sum(old * old, axis=-1, keepdims=True)) + 1e-06)
    moved_norm = jnp.sqrt(lax.optimization_barrier(jnp.sum(moved * moved, axis=-1, keepdims=True)) + 1e-06)
    return moved * old_norm / moved_norm

def reference(query_tokens, key_tokens, value_tokens, learn_rates, fast_first, fast_third, fast_second, momentum_decay):
    start_low = (fast_first, fast_third, fast_second)
    weights0 = tuple((w.astype(jnp.float32) for w in start_low))
    out_zero = apply_all(start_low, query_tokens[0])
    step0 = step_all(start_low, key_tokens[0], value_tokens[0], learn_rates[0])
    step1 = step_all(start_low, key_tokens[1], value_tokens[1], learn_rates[1])
    weights1 = tuple((renorm(w, w + m) for w, m in zip(weights0, step0)))
    low_one = tuple((w.astype(jnp.bfloat16) for w in weights1))
    out_one = apply_all(low_one, query_tokens[1])
    decay = momentum_decay[:, None, None]
    mom2 = tuple((decay * m + s for m, s in zip(step0, step1)))
    weights2 = tuple((renorm(w, w + m) for w, m in zip(weights1, mom2)))
    low_two = tuple((w.astype(jnp.bfloat16) for w in weights2))
    out_two = apply_all(low_two, query_tokens[2])
    return jnp.stack([out_zero, out_one, out_two]).astype(jnp.bfloat16)
```

```python
import jax
import jax.numpy as jnp
from jax import lax
from jax.experimental import pallas as pl
from jax.experimental.pallas import tpu as pltpu
from jax.sharding import PartitionSpec as P

MESH = pl.DeviceIdType.MESH


def forward_parts(weights, inputs):
    first, third, second = weights
    length = inputs.shape[0]
    head_count = first.shape[0]
    shaped = inputs.reshape(length, head_count, -1)
    pre_gate = jnp.einsum("thd,hfd->htf", shaped, first, preferred_element_type=jnp.float32)
    pre_up = jnp.einsum("thd,hfd->htf", shaped, third, preferred_element_type=jnp.float32)
    hidden = (jax.nn.silu(pre_gate) * pre_up).astype(jnp.bfloat16)
    return (shaped, pre_gate, pre_up, hidden)


def apply_block(weights, inputs):
    shaped, pre_gate, pre_up, hidden = forward_parts(weights, inputs)
    result = jnp.einsum("htf,hdf->thd", hidden, weights[2], preferred_element_type=jnp.float32)
    return result.reshape(inputs.shape[0], -1).astype(jnp.bfloat16)


def partial_steps(weights, keys, values, rates):
    shaped, pre_gate, pre_up, hidden = forward_parts(weights, keys)
    length = keys.shape[0]
    head_count = weights[0].shape[0]
    scaled = (
        rates[:, :, None] * values.reshape(length, head_count, -1).astype(jnp.float32)
    ).astype(jnp.bfloat16)
    step_second = jnp.einsum("thd,htf->hdf", scaled, hidden, preferred_element_type=jnp.float32)
    back = jnp.einsum("thd,hdf->htf", scaled, weights[2], preferred_element_type=jnp.float32)
    sig_gate = jax.nn.sigmoid(pre_gate)
    d_gate = (back * pre_up * sig_gate * (1.0 + pre_gate * (1.0 - sig_gate))).astype(jnp.bfloat16)
    d_up = (back * pre_gate * sig_gate).astype(jnp.bfloat16)
    step_first = jnp.einsum("htf,thd->hfd", d_gate, shaped, preferred_element_type=jnp.float32)
    step_third = jnp.einsum("htf,thd->hfd", d_up, shaped, preferred_element_type=jnp.float32)
    return (step_first, step_third, step_second)


def renorm(old, moved):
    old_norm = jnp.sqrt(jnp.sum(old * old, axis=-1, keepdims=True) + 1e-06)
    moved_norm = jnp.sqrt(jnp.sum(moved * moved, axis=-1, keepdims=True) + 1e-06)
    return moved * old_norm / moved_norm


def shards(
    query_tokens,
    key_tokens,
    value_tokens,
    learn_rates,
    fast_first,
    fast_third,
    fast_second,
    momentum_decay,
):
    owned_zero = jnp.stack([fast_first, fast_third, fast_second])
    full_zero = lax.all_gather(owned_zero, "tok", axis=2, tiled=True)
    terms_zero = partial_steps(full_zero, key_tokens[0], value_tokens[0], learn_rates[0])
    terms_one = partial_steps(full_zero, key_tokens[1], value_tokens[1], learn_rates[1])
    step_zero = lax.psum_scatter(
        jnp.stack(terms_zero).astype(jnp.bfloat16), "tok", scatter_dimension=2, tiled=True
    ).astype(jnp.float32)
    step_one = lax.psum_scatter(
        jnp.stack(terms_one).astype(jnp.bfloat16), "tok", scatter_dimension=2, tiled=True
    ).astype(jnp.float32)
    out_zero = apply_block(full_zero, query_tokens[0])
    decay = momentum_decay[None, :, None, None]
    weights_zero = owned_zero.astype(jnp.float32)
    weights_one = renorm(weights_zero, weights_zero + step_zero)
    full_one = lax.all_gather(weights_one.astype(jnp.bfloat16), "tok", axis=2, tiled=True)
    weights_two = renorm(weights_one, weights_one + decay * step_zero + step_one)
    full_two = lax.all_gather(weights_two.astype(jnp.bfloat16), "tok", axis=2, tiled=True)
    out_one = apply_block(full_one, query_tokens[1])
    out_two = apply_block(full_two, query_tokens[2])
    return jnp.stack([out_zero, out_one, out_two])


def dot_nt(a, b):
    return lax.dot_general(a, b, (((1,), (1,)), ((), ())), preferred_element_type=jnp.float32)


def dot_nn(a, b):
    return lax.dot_general(a, b, (((1,), (0,)), ((), ())), preferred_element_type=jnp.float32)


def dot_tn(a, b):
    return lax.dot_general(a, b, (((0,), (0,)), ((), ())), preferred_element_type=jnp.float32)


def kernel(
    query_ref,
    key_ref,
    value_ref,
    rate_ref,
    first_ref,
    third_ref,
    second_ref,
    decay_ref,
    out_ref,
    queries,
    keys,
    values,
    rates,
    full,
    part,
    core_out,
    core_in,
    side_out,
    side_in,
    far_out,
    far_in,
    step_own,
    weight_own,
    result,
    gates,
    ups,
    hiddens,
    swap_send,
    swap_recv,
    local_sem,
    gather_send,
    gather_recv,
    first_send,
    first_recv,
    first_local,
    sum_send,
    sum_recv,
    out_send,
    out_recv,
    out_local,
):
    index = lax.axis_index("tok")
    core = index % 2
    lane = (index // 2) % 2
    head = (index // 4) % 2
    pair = index // 8
    group = lax.axis_index("groups")
    across = {"groups": 1 - group}
    partner = {"tok": index + 1 - 2 * core}
    beside = {"tok": index + 2 - 4 * lane}
    mate = {"tok": index + 4 - 8 * head}
    beyond = {"tok": index + 8 - 16 * pair}
    crossed = {"tok": index + 12 - 8 * head - 16 * pair}
    corner = {"groups": 1 - group, "tok": index + 2 - 4 * lane}
    rows = first_ref.shape[1]
    tokens = key_ref.shape[1]
    width = first_ref.shape[2]
    hidden_units = 16 * rows

    barrier = pltpu.get_barrier_semaphore()
    others = (crossed, beyond, corner, mate, beside, across, partner)
    for other in others:
        pl.semaphore_signal(barrier, inc=1, device_id=other, device_id_type=MESH)
    pl.semaphore_wait(barrier, len(others))

    sent = []

    def push(src, dst, send_sem, recv_sem, to):
        return pltpu.make_async_remote_copy(
            src_ref=src,
            dst_ref=dst,
            send_sem=send_sem,
            recv_sem=recv_sem,
            device_id=to,
            device_id_type=MESH,
        )

    def go(copy):
        copy.start()
        sent.append(copy)

    mine = pl.ds(pl.multiple_of(head * width, width), width)
    theirs = pl.ds(pl.multiple_of((1 - head) * width, width), width)
    slot = pl.ds(pl.multiple_of(head * tokens, tokens), tokens)
    other_slot = pl.ds(pl.multiple_of((1 - head) * tokens, tokens), tokens)

    pairs = []
    for b in range(2):
        pairs.append((key_ref.at[b, :, theirs], key_ref.at[b, :, mine], keys.at[b, slot, :]))
        pairs.append((value_ref.at[b, :, theirs], value_ref.at[b, :, mine], values.at[b, slot, :]))
        pairs.append((rate_ref.at[b], rate_ref.at[b], rates.at[b, :, slot]))
    for b in range(3):
        pairs.append((query_ref.at[b, :, theirs], query_ref.at[b, :, mine], queries.at[b, slot, :]))
    swaps = {}
    locals_ = {}

    def swap(first, last):
        for n in range(first, last):
            away, here, target = pairs[n]
            swaps[n] = push(away, target, swap_send.at[n], swap_recv.at[n], mate)
            swaps[n].start()
            locals_[n] = pltpu.make_async_copy(here, target, local_sem.at[n])
            locals_[n].start()

    def ready(n):
        swaps[n].wait_recv()
        locals_[n].wait()

    def block_of(k, m, p, q):
        return full.at[k, m, p, :, q, core]

    def gather_copy(k, m, n):
        p, q = (
            (pair, lane),
            (pair, lane),
            (1 - pair, lane),
            (pair, lane),
            (1 - pair, lane),
            (pair, 1 - lane),
            (1 - pair, 1 - lane),
        )[n]
        span = block_of(k, m, p, q)
        to = (beyond, beside, beside, partner, partner, partner, partner)[n]
        return push(span, span, gather_send.at[k - 1, m, n], gather_recv.at[k - 1, m, n], to)

    share = pl.ds(pl.multiple_of(group * (width // 2), width // 2), width // 2)
    initial = (first_ref, third_ref, second_ref)

    def first_copy(m, n):
        ref = initial[m]
        own = full.at[0, m, pair, head, lane, core]
        near = full.at[0, m, pair, 1 - head, lane, core]
        wide = full.at[0, m, 1 - pair, :, lane, core, :, share]
        src, dst, to = (
            (ref.at[1 - head], own, mate),
            (ref.at[head, :, share], own.at[:, share], beyond),
            (ref.at[1 - head, :, share], own.at[:, share], crossed),
            (ref.at[head], own, beside),
            (ref.at[head], own, partner),
            (near, near, beside),
            (near, near, partner),
            (wide, wide, beside),
            (wide, wide, across),
            (wide, wide, corner),
            (block_of(0, m, pair, 1 - lane),) * 2 + (partner,),
            (block_of(0, m, 1 - pair, lane),) * 2 + (partner,),
            (block_of(0, m, 1 - pair, 1 - lane),) * 2 + (partner,),
        )[n]
        return push(src, dst, first_send.at[m, n], first_recv.at[m, n], to)

    def first_here(m):
        return pltpu.make_async_copy(
            initial[m].at[head], full.at[0, m, pair, head, lane, core], first_local.at[m]
        )

    def first_start():
        for m in range(3):
            for n in (2, 1, 0, 3, 4):
                go(first_copy(m, n))
            first_here(m).start()

    def first_spread():
        for m in range(3):
            first_copy(m, 0).wait_recv()
            go(first_copy(m, 5))
            go(first_copy(m, 6))
        for m in range(3):
            first_copy(m, 2).wait_recv()
            first_copy(m, 1).wait_recv()
            for n in (7, 9, 8):
                go(first_copy(m, n))
        for m in range(3):
            first_copy(m, 3).wait_recv()
            first_copy(m, 5).wait_recv()
            go(first_copy(m, 10))
        for m in range(3):
            first_copy(m, 8).wait_recv()
            go(first_copy(m, 11))
            first_copy(m, 7).wait_recv()
            first_copy(m, 9).wait_recv()
            go(first_copy(m, 12))

    def first_end(m):
        first_here(m).wait()
        for n in (4, 6, 10, 11, 12):
            first_copy(m, n).wait_recv()

    def gather_own(k, m):
        for n in (0, 1, 3):
            go(gather_copy(k, m, n))

    def gather_beyond(k, m):
        gather_copy(k, m, 0).wait_recv()
        go(gather_copy(k, m, 2))
        go(gather_copy(k, m, 4))

    def gather_beside(k, m, n):
        gather_copy(k, m, n).wait_recv()
        go(gather_copy(k, m, n + 4))

    def gather_end(k, m):
        for n in range(3, 7):
            gather_copy(k, m, n).wait_recv()

    def core_copy(t):
        return push(
            core_out.at[t], core_in.at[t], sum_send.at[t, 0], sum_recv.at[t, 0], partner
        )

    def side_copy(t, p, n):
        return push(
            side_out.at[t, p], side_in.at[t, p], sum_send.at[t, n], sum_recv.at[t, n], beside
        )

    def far_copy(t):
        return push(far_out.at[t], far_in.at[t], sum_send.at[t, 3], sum_recv.at[t, 3], beyond)

    def core_start(t):
        core_out[t] = part[t, :, :, :, 1 - core].astype(jnp.bfloat16)
        go(core_copy(t))

    def core_sum(t, p, q):
        return part[t, p, :, q, core] + core_in[t, p, :, q].astype(jnp.float32)

    def side_start(ts):
        for n in (1, 2):
            for t in ts:
                if n == 1:
                    core_copy(t).wait_recv()
                p = 1 - pair if n == 1 else pair
                side_out[t, p] = core_sum(t, p, 1 - lane).astype(jnp.bfloat16)
                go(side_copy(t, p, n))

    def far_start(t):
        p = 1 - pair
        side_copy(t, p, 1).wait_recv()
        far_out[t] = (core_sum(t, p, lane) + side_in[t, p].astype(jnp.float32)).astype(
            jnp.bfloat16
        )
        go(far_copy(t))

    def total_of(t):
        side_copy(t, pair, 2).wait_recv()
        near = core_sum(t, pair, lane) + side_in[t, pair].astype(jnp.float32)
        far_copy(t).wait_recv()
        return near + far_in[t].astype(jnp.float32)

    order = (2, 0, 1)

    def whole(k, m):
        return full[k, m].reshape(hidden_units, width)

    def forward(k, x):
        gate = dot_nt(x, whole(k, 0))
        up = dot_nt(x, whole(k, 1))
        sig = jax.nn.sigmoid(gate)
        return gate, up, sig, (gate * sig * up).astype(jnp.bfloat16)

    def keys_forward(j):
        gate, up, sig, hidden = forward(0, keys[j])
        gates[...] = gate
        ups[...] = up
        hiddens[...] = hidden

    def steps(j):
        row = jnp.where(head == 0, rates[j, 0:1, :], rates[j, 1:2, :])
        rate = jnp.transpose(jnp.broadcast_to(row, (128, row.shape[1])))[:, 0:1]
        scaled = (rate * values[j].astype(jnp.float32)).astype(jnp.bfloat16)
        part[3 * j + 2] = dot_tn(scaled, hiddens[...]).reshape(part.shape[1:])
        core_start(3 * j + 2)
        if j == 0:
            first_end(2)
        back = dot_nn(scaled, whole(0, 2))
        gate = gates[...]
        sig = jax.nn.sigmoid(gate)
        x = keys[j]
        d_gate = (back * ups[...] * sig * (1.0 + gate * (1.0 - sig))).astype(jnp.bfloat16)
        part[3 * j] = dot_tn(d_gate, x).reshape(part.shape[1:])
        core_start(3 * j)
        d_up = (back * gate * sig).astype(jnp.bfloat16)
        part[3 * j + 1] = dot_tn(d_up, x).reshape(part.shape[1:])
        core_start(3 * j + 1)

    outs = []

    def read_hidden(k):
        gate, up, sig, hidden = forward(k, queries[k])
        hiddens[...] = hidden

    def read_out(k):
        result[k] = dot_nt(hiddens[...], whole(k, 2)).astype(jnp.bfloat16)
        away = push(
            result.at[k, other_slot, :],
            out_ref.at[k, :, mine],
            out_send.at[k],
            out_recv.at[k],
            mate,
        )
        away.start()
        here = pltpu.make_async_copy(
            result.at[k, slot, :], out_ref.at[k, :, mine], out_local.at[k]
        )
        here.start()
        outs.append((away, here))

    first_start()
    swap(0, 6)
    first_spread()
    for m in range(2):
        first_end(m)
    for n in range(0, 3):
        ready(n)
    keys_forward(0)
    steps(0)
    side_start(order)
    for n in range(3, 6):
        ready(n)
    keys_forward(1)
    steps(1)
    for m in order:
        far_start(m)
    side_start([3 + m for m in order])
    swap(6, 7)
    for m in order:
        moment = total_of(m)
        step_own[m] = moment
        old = full[0, m, pair, :, lane, core].astype(jnp.float32)
        fresh = renorm(old, old + moment)
        weight_own[m] = fresh
        full[1, m, pair, :, lane, core] = fresh.astype(jnp.bfloat16)
        gather_own(1, m)
    decay = decay_ref[head]
    for m in order:
        far_start(3 + m)
    swap(7, 8)
    for m in order:
        gather_beyond(1, m)
        gather_beside(1, m, 1)
    ready(6)
    read_hidden(0)
    read_out(0)
    for m in order:
        moment = decay * step_own[m] + total_of(3 + m)
        old = weight_own[m]
        fresh = renorm(old, old + moment)
        full[2, m, pair, :, lane, core] = fresh.astype(jnp.bfloat16)
        gather_own(2, m)
    swap(8, 9)
    for m in order:
        gather_beside(1, m, 2)
    for m in order:
        gather_beyond(2, m)
        gather_beside(2, m, 1)
    for m in range(3):
        gather_end(1, m)
    ready(7)
    read_hidden(1)
    read_out(1)
    ready(8)
    for m in order:
        gather_beside(2, m, 2)
    gather_end(2, 2)
    gather_end(2, 0)
    gates[...] = dot_nt(queries[2], whole(2, 0))
    gather_end(2, 1)
    gate = gates[...]
    up = dot_nt(queries[2], whole(2, 1))
    hiddens[...] = (gate * jax.nn.sigmoid(gate) * up).astype(jnp.bfloat16)
    read_out(2)

    for n in range(len(pairs)):
        swaps[n].wait_send()
    for copy in sent:
        copy.wait_send()
    for away, here in outs:
        here.wait()
        away.wait()


def fused_shards(query, key, value, rate, first, third, second, decay):
    blocks, tokens, features = query.shape
    heads, rows, width = first.shape
    hidden = 16 * rows
    span = 2 * tokens
    anywhere = pl.BlockSpec(memory_space=pl.ANY)
    dma = pltpu.SemaphoreType.DMA
    low, wide = jnp.bfloat16, jnp.float32
    return pl.pallas_call(
        kernel,
        out_shape=jax.ShapeDtypeStruct(query.shape, low),
        in_specs=[anywhere] * 7 + [pl.BlockSpec(memory_space=pltpu.SMEM)],
        out_specs=anywhere,
        scratch_shapes=[
            pltpu.VMEM((3, span, width), low),
            pltpu.VMEM((2, span, width), low),
            pltpu.VMEM((2, span, width), low),
            pltpu.VMEM((2, heads, span), wide),
            pltpu.VMEM((3, 3, 2, 2, 2, 2, rows, width), low),
            pltpu.VMEM((6, 2, 2, 2, 2, rows, width), wide),
            pltpu.VMEM((6, 2, 2, 2, rows, width), low),
            pltpu.VMEM((6, 2, 2, 2, rows, width), low),
            pltpu.VMEM((6, 2, 2, rows, width), low),
            pltpu.VMEM((6, 2, 2, rows, width), low),
            pltpu.VMEM((6, 2, rows, width), low),
            pltpu.VMEM((6, 2, rows, width), low),
            pltpu.VMEM((3, 2, rows, width), wide),
            pltpu.VMEM((3, 2, rows, width), wide),
            pltpu.VMEM((3, span, width), low),
            pltpu.VMEM((span, hidden), wide),
            pltpu.VMEM((span, hidden), wide),
            pltpu.VMEM((span, hidden), low),
            dma((9,)),
            dma((9,)),
            dma((9,)),
            dma((2, 3, 7)),
            dma((2, 3, 7)),
            dma((3, 13)),
            dma((3, 13)),
            dma((3,)),
            dma((6, 4)),
            dma((6, 4)),
            dma((3,)),
            dma((3,)),
            dma((3,)),
        ],
        compiler_params=pltpu.CompilerParams(
            collective_id=0, has_side_effects=True, vmem_limit_bytes=60 * 1024 * 1024
        ),
    )(query, key, value, jnp.swapaxes(rate, 1, 2), first, third, second, decay)


def solution(mesh):
    placed = (
        P(None, ("groups", "tok"), None),
        P(None, ("groups", "tok"), None),
        P(None, ("groups", "tok"), None),
        P(None, ("groups", "tok"), None),
        P(None, "tok", None),
        P(None, "tok", None),
        P(None, "tok", None),
        P(),
    )
    chips = mesh.shape["tok"] // 2

    def body(*arrays):
        rows = arrays[4].shape[1]
        if rows % 16 or chips != 8 or arrays[4].shape[0] != 2 or mesh.shape["groups"] != 2:
            return shards(*arrays)
        return fused_shards(*arrays)

    return jax.shard_map(
        body,
        mesh=mesh,
        in_specs=placed,
        out_specs=P(None, ("groups", "tok"), None),
        check_vma=False,
    )
```

```python
import jax
import jax.numpy as jnp
from jax import lax
from jax.experimental import pallas as pl
from jax.experimental.pallas import tpu as pltpu
from jax.sharding import PartitionSpec as P

MESH = pl.DeviceIdType.MESH


def forward_parts(weights, inputs):
    first, third, second = weights
    length = inputs.shape[0]
    head_count = first.shape[0]
    shaped = inputs.reshape(length, head_count, -1)
    pre_gate = jnp.einsum("thd,hfd->htf", shaped, first, preferred_element_type=jnp.float32)
    pre_up = jnp.einsum("thd,hfd->htf", shaped, third, preferred_element_type=jnp.float32)
    hidden = (jax.nn.silu(pre_gate) * pre_up).astype(jnp.bfloat16)
    return (shaped, pre_gate, pre_up, hidden)


def apply_block(weights, inputs):
    shaped, pre_gate, pre_up, hidden = forward_parts(weights, inputs)
    result = jnp.einsum("htf,hdf->thd", hidden, weights[2], preferred_element_type=jnp.float32)
    return result.reshape(inputs.shape[0], -1).astype(jnp.bfloat16)


def partial_steps(weights, keys, values, rates):
    shaped, pre_gate, pre_up, hidden = forward_parts(weights, keys)
    length = keys.shape[0]
    head_count = weights[0].shape[0]
    scaled = (
        rates[:, :, None] * values.reshape(length, head_count, -1).astype(jnp.float32)
    ).astype(jnp.bfloat16)
    step_second = jnp.einsum("thd,htf->hdf", scaled, hidden, preferred_element_type=jnp.float32)
    back = jnp.einsum("thd,hdf->htf", scaled, weights[2], preferred_element_type=jnp.float32)
    sig_gate = jax.nn.sigmoid(pre_gate)
    d_gate = (back * pre_up * sig_gate * (1.0 + pre_gate * (1.0 - sig_gate))).astype(jnp.bfloat16)
    d_up = (back * pre_gate * sig_gate).astype(jnp.bfloat16)
    step_first = jnp.einsum("htf,thd->hfd", d_gate, shaped, preferred_element_type=jnp.float32)
    step_third = jnp.einsum("htf,thd->hfd", d_up, shaped, preferred_element_type=jnp.float32)
    return (step_first, step_third, step_second)


def renorm(old, moved):
    old_norm = jnp.sqrt(jnp.sum(old * old, axis=-1, keepdims=True) + 1e-06)
    moved_norm = jnp.sqrt(jnp.sum(moved * moved, axis=-1, keepdims=True) + 1e-06)
    return moved * old_norm / moved_norm


def shards(
    query_tokens,
    key_tokens,
    value_tokens,
    learn_rates,
    fast_first,
    fast_third,
    fast_second,
    momentum_decay,
):
    owned_zero = jnp.stack([fast_first, fast_third, fast_second])
    full_zero = lax.all_gather(owned_zero, "tok", axis=2, tiled=True)
    terms_zero = partial_steps(full_zero, key_tokens[0], value_tokens[0], learn_rates[0])
    terms_one = partial_steps(full_zero, key_tokens[1], value_tokens[1], learn_rates[1])
    step_zero = lax.psum_scatter(
        jnp.stack(terms_zero).astype(jnp.bfloat16), "tok", scatter_dimension=2, tiled=True
    ).astype(jnp.float32)
    step_one = lax.psum_scatter(
        jnp.stack(terms_one).astype(jnp.bfloat16), "tok", scatter_dimension=2, tiled=True
    ).astype(jnp.float32)
    out_zero = apply_block(full_zero, query_tokens[0])
    decay = momentum_decay[None, :, None, None]
    weights_zero = owned_zero.astype(jnp.float32)
    weights_one = renorm(weights_zero, weights_zero + step_zero)
    full_one = lax.all_gather(weights_one.astype(jnp.bfloat16), "tok", axis=2, tiled=True)
    weights_two = renorm(weights_one, weights_one + decay * step_zero + step_one)
    full_two = lax.all_gather(weights_two.astype(jnp.bfloat16), "tok", axis=2, tiled=True)
    out_one = apply_block(full_one, query_tokens[1])
    out_two = apply_block(full_two, query_tokens[2])
    return jnp.stack([out_zero, out_one, out_two])


def dot_nt(a, b):
    return lax.dot_general(a, b, (((1,), (1,)), ((), ())), preferred_element_type=jnp.float32)


def dot_nn(a, b):
    return lax.dot_general(a, b, (((1,), (0,)), ((), ())), preferred_element_type=jnp.float32)


def dot_tn(a, b):
    return lax.dot_general(a, b, (((0,), (0,)), ((), ())), preferred_element_type=jnp.float32)


def kernel(
    query_ref,
    key_ref,
    value_ref,
    rate_ref,
    first_ref,
    third_ref,
    second_ref,
    decay_ref,
    out_ref,
    queries,
    keys,
    values,
    rates,
    full,
    part,
    core_out,
    core_in,
    side_out,
    side_in,
    far_out,
    far_in,
    step_own,
    weight_own,
    result,
    gates,
    ups,
    hiddens,
    swap_send,
    swap_recv,
    local_sem,
    gather_send,
    gather_recv,
    first_send,
    first_recv,
    first_local,
    rows_here,
    sum_send,
    sum_recv,
    out_send,
    out_recv,
    out_local,
):
    index = lax.axis_index("tok")
    core = index % 2
    lane = (index // 2) % 2
    head = (index // 4) % 2
    pair = index // 8
    group = lax.axis_index("groups")
    across = {"groups": 1 - group}
    partner = {"tok": index + 1 - 2 * core}
    beside = {"tok": index + 2 - 4 * lane}
    mate = {"tok": index + 4 - 8 * head}
    beyond = {"tok": index + 8 - 16 * pair}
    crossed = {"tok": index + 12 - 8 * head - 16 * pair}
    corner = {"groups": 1 - group, "tok": index + 2 - 4 * lane}
    rows = first_ref.shape[1]
    tokens = key_ref.shape[1]
    width = first_ref.shape[2]
    hidden_units = 16 * rows

    for m, ref in enumerate((first_ref, third_ref, second_ref)):
        pltpu.make_async_copy(ref, rows_here.at[m], first_local.at[m]).start()

    barrier = pltpu.get_barrier_semaphore()
    others = (crossed, beyond, corner, mate, beside, across, partner)
    for other in others:
        pl.semaphore_signal(barrier, inc=1, device_id=other, device_id_type=MESH)
    pl.semaphore_wait(barrier, len(others))

    sent = []

    def push(src, dst, send_sem, recv_sem, to):
        return pltpu.make_async_remote_copy(
            src_ref=src,
            dst_ref=dst,
            send_sem=send_sem,
            recv_sem=recv_sem,
            device_id=to,
            device_id_type=MESH,
        )

    def go(copy):
        copy.start()
        sent.append(copy)

    mine = pl.ds(pl.multiple_of(head * width, width), width)
    theirs = pl.ds(pl.multiple_of((1 - head) * width, width), width)
    slot = pl.ds(pl.multiple_of(head * tokens, tokens), tokens)
    other_slot = pl.ds(pl.multiple_of((1 - head) * tokens, tokens), tokens)

    pairs = []
    for b in range(2):
        pairs.append((key_ref.at[b, :, theirs], key_ref.at[b, :, mine], keys.at[b, slot, :]))
        pairs.append((value_ref.at[b, :, theirs], value_ref.at[b, :, mine], values.at[b, slot, :]))
        pairs.append((rate_ref.at[b], rate_ref.at[b], rates.at[b, :, slot]))
    for b in range(3):
        pairs.append((query_ref.at[b, :, theirs], query_ref.at[b, :, mine], queries.at[b, slot, :]))
    swaps = {}
    locals_ = {}

    def swap(first, last):
        for n in range(first, last):
            away, here, target = pairs[n]
            swaps[n] = push(away, target, swap_send.at[n], swap_recv.at[n], mate)
            swaps[n].start()
            locals_[n] = pltpu.make_async_copy(here, target, local_sem.at[n])
            locals_[n].start()

    def ready(n):
        swaps[n].wait_recv()
        locals_[n].wait()

    def block_of(k, m, p, q):
        return full.at[k, m, p, :, q, core]

    def gather_copy(k, m, n):
        p, q = (
            (pair, lane),
            (pair, lane),
            (1 - pair, lane),
            (pair, lane),
            (1 - pair, lane),
            (pair, 1 - lane),
            (1 - pair, 1 - lane),
        )[n]
        span = block_of(k, m, p, q)
        to = (beyond, beside, beside, partner, partner, partner, partner)[n]
        return push(span, span, gather_send.at[k - 1, m, n], gather_recv.at[k - 1, m, n], to)

    share = pl.ds(pl.multiple_of(group * (width // 2), width // 2), width // 2)

    def first_copy(m, n):
        ref = rows_here.at[m]
        own = full.at[0, m, pair, head, lane, core]
        near = full.at[0, m, pair, 1 - head, lane, core]
        wide = full.at[0, m, 1 - pair, :, lane, core, :, share]
        src, dst, to = (
            (ref.at[1 - head, :, share], own.at[:, share], mate),
            (ref.at[head, :, share], own.at[:, share], beyond),
            (ref.at[1 - head, :, share], own.at[:, share], crossed),
            (ref.at[head], own, beside),
            (ref.at[head], own, partner),
            (near.at[:, share], near.at[:, share], beside),
            (near.at[:, share], near.at[:, share], across),
            (wide, wide, beside),
            (wide, wide, across),
            (wide, wide, corner),
            (near.at[:, share], near.at[:, share], corner),
            (near, near, partner),
            (block_of(0, m, pair, 1 - lane),) * 2 + (partner,),
            (block_of(0, m, 1 - pair, lane),) * 2 + (partner,),
            (block_of(0, m, 1 - pair, 1 - lane),) * 2 + (partner,),
        )[n]
        return push(src, dst, first_send.at[m, n], first_recv.at[m, n], to)

    def first_here(m):
        return pltpu.make_async_copy(
            rows_here.at[m, head], full.at[0, m, pair, head, lane, core], first_local.at[m]
        )

    def first_start():
        for m, ref in enumerate((first_ref, third_ref, second_ref)):
            pltpu.make_async_copy(ref, rows_here.at[m], first_local.at[m]).wait()
        for m in range(3):
            for n in (2, 1, 0, 3, 4):
                go(first_copy(m, n))
            first_here(m).start()

    def first_spread():
        for m in range(3):
            first_copy(m, 0).wait_recv()
            for n in (5, 10, 6):
                go(first_copy(m, n))
        for m in range(3):
            first_copy(m, 2).wait_recv()
            first_copy(m, 1).wait_recv()
            for n in (7, 9, 8):
                go(first_copy(m, n))
        for m in range(3):
            first_copy(m, 6).wait_recv()
            go(first_copy(m, 11))
            for n in (3, 5, 10):
                first_copy(m, n).wait_recv()
            go(first_copy(m, 12))
        for m in range(3):
            first_copy(m, 8).wait_recv()
            go(first_copy(m, 13))
            first_copy(m, 7).wait_recv()
            first_copy(m, 9).wait_recv()
            go(first_copy(m, 14))

    def first_end(m):
        first_here(m).wait()
        for n in (4, 11, 12, 13, 14):
            first_copy(m, n).wait_recv()

    def gather_own(k, m):
        for n in (0, 1, 3):
            go(gather_copy(k, m, n))

    def gather_beyond(k, m):
        gather_copy(k, m, 0).wait_recv()
        go(gather_copy(k, m, 2))
        go(gather_copy(k, m, 4))

    def gather_beside(k, m, n):
        gather_copy(k, m, n).wait_recv()
        go(gather_copy(k, m, n + 4))

    def gather_end(k, m):
        for n in range(3, 7):
            gather_copy(k, m, n).wait_recv()

    def core_copy(t):
        return push(
            core_out.at[t], core_in.at[t], sum_send.at[t, 0], sum_recv.at[t, 0], partner
        )

    def side_copy(t, p, n):
        return push(
            side_out.at[t, p], side_in.at[t, p], sum_send.at[t, n], sum_recv.at[t, n], beside
        )

    def far_copy(t):
        return push(far_out.at[t], far_in.at[t], sum_send.at[t, 3], sum_recv.at[t, 3], beyond)

    def core_start(t):
        core_out[t] = part[t, :, :, :, 1 - core].astype(jnp.bfloat16)
        go(core_copy(t))

    def core_sum(t, p, q):
        return part[t, p, :, q, core] + core_in[t, p, :, q].astype(jnp.float32)

    def side_start(ts):
        for n in (1, 2):
            for t in ts:
                if n == 1:
                    core_copy(t).wait_recv()
                p = 1 - pair if n == 1 else pair
                side_out[t, p] = core_sum(t, p, 1 - lane).astype(jnp.bfloat16)
                go(side_copy(t, p, n))

    def far_start(t):
        p = 1 - pair
        side_copy(t, p, 1).wait_recv()
        far_out[t] = (core_sum(t, p, lane) + side_in[t, p].astype(jnp.float32)).astype(
            jnp.bfloat16
        )
        go(far_copy(t))

    def total_of(t):
        side_copy(t, pair, 2).wait_recv()
        near = core_sum(t, pair, lane) + side_in[t, pair].astype(jnp.float32)
        far_copy(t).wait_recv()
        return near + far_in[t].astype(jnp.float32)

    order = (2, 0, 1)

    def whole(k, m):
        return full[k, m].reshape(hidden_units, width)

    def forward(k, x):
        gate = dot_nt(x, whole(k, 0))
        up = dot_nt(x, whole(k, 1))
        sig = jax.nn.sigmoid(gate)
        return gate, up, sig, (gate * sig * up).astype(jnp.bfloat16)

    def keys_forward(j):
        gate, up, sig, hidden = forward(0, keys[j])
        gates[...] = gate
        ups[...] = up
        hiddens[...] = hidden

    def steps(j):
        row = jnp.where(head == 0, rates[j, 0:1, :], rates[j, 1:2, :])
        rate = jnp.transpose(jnp.broadcast_to(row, (128, row.shape[1])))[:, 0:1]
        scaled = (rate * values[j].astype(jnp.float32)).astype(jnp.bfloat16)
        part[3 * j + 2] = dot_tn(scaled, hiddens[...]).reshape(part.shape[1:])
        core_start(3 * j + 2)
        if j == 0:
            first_end(2)
        back = dot_nn(scaled, whole(0, 2))
        gate = gates[...]
        sig = jax.nn.sigmoid(gate)
        x = keys[j]
        d_gate = (back * ups[...] * sig * (1.0 + gate * (1.0 - sig))).astype(jnp.bfloat16)
        part[3 * j] = dot_tn(d_gate, x).reshape(part.shape[1:])
        core_start(3 * j)
        d_up = (back * gate * sig).astype(jnp.bfloat16)
        part[3 * j + 1] = dot_tn(d_up, x).reshape(part.shape[1:])
        core_start(3 * j + 1)

    outs = []

    def read_hidden(k):
        gate, up, sig, hidden = forward(k, queries[k])
        hiddens[...] = hidden

    def read_out(k):
        result[k] = dot_nt(hiddens[...], whole(k, 2)).astype(jnp.bfloat16)
        send_out(k)
        keep_out(k)

    def send_out(k):
        away = push(
            result.at[k, other_slot, :],
            out_ref.at[k, :, mine],
            out_send.at[k],
            out_recv.at[k],
            mate,
        )
        away.start()
        outs.append(away)

    def keep_out(k):
        here = pltpu.make_async_copy(
            result.at[k, slot, :], out_ref.at[k, :, mine], out_local.at[k]
        )
        here.start()
        outs.append(here)

    first_start()
    swap(0, 6)
    first_spread()
    for m in range(2):
        first_end(m)
    for n in range(0, 3):
        ready(n)
    keys_forward(0)
    steps(0)
    side_start(order)
    for n in range(3, 6):
        ready(n)
    keys_forward(1)
    steps(1)
    for m in order:
        far_start(m)
    side_start([3 + m for m in order])
    swap(6, 7)
    for m in order:
        moment = total_of(m)
        step_own[m] = moment
        old = full[0, m, pair, :, lane, core].astype(jnp.float32)
        fresh = renorm(old, old + moment)
        weight_own[m] = fresh
        full[1, m, pair, :, lane, core] = fresh.astype(jnp.bfloat16)
        gather_own(1, m)
    decay = decay_ref[head]
    for m in order:
        far_start(3 + m)
    swap(7, 8)
    for m in order:
        gather_beyond(1, m)
        gather_beside(1, m, 1)
    ready(6)
    read_hidden(0)
    read_out(0)
    for m in order:
        moment = decay * step_own[m] + total_of(3 + m)
        old = weight_own[m]
        fresh = renorm(old, old + moment)
        full[2, m, pair, :, lane, core] = fresh.astype(jnp.bfloat16)
        gather_own(2, m)
    swap(8, 9)
    for m in order:
        gather_beside(1, m, 2)
    for m in order:
        gather_beyond(2, m)
        gather_beside(2, m, 1)
    for m in range(3):
        gather_end(1, m)
    ready(7)
    read_hidden(1)
    read_out(1)
    ready(8)
    for m in order:
        gather_beside(2, m, 2)
    gather_end(2, 2)
    gather_end(2, 0)
    gates[...] = dot_nt(queries[2], whole(2, 0))
    gather_end(2, 1)
    for place in (other_slot, slot):
        gate = gates[place, :]
        up = dot_nt(queries[2, place, :], whole(2, 1))
        hidden = (gate * jax.nn.sigmoid(gate) * up).astype(jnp.bfloat16)
        result[2, place, :] = dot_nt(hidden, whole(2, 2)).astype(jnp.bfloat16)
        if place is other_slot:
            send_out(2)
    keep_out(2)

    for n in range(len(pairs)):
        swaps[n].wait_send()
    for copy in sent:
        copy.wait_send()
    for copy in outs:
        copy.wait()


def fused_shards(query, key, value, rate, first, third, second, decay):
    blocks, tokens, features = query.shape
    heads, rows, width = first.shape
    hidden = 16 * rows
    span = 2 * tokens
    anywhere = pl.BlockSpec(memory_space=pl.ANY)
    dma = pltpu.SemaphoreType.DMA
    low, wide = jnp.bfloat16, jnp.float32
    return pl.pallas_call(
        kernel,
        out_shape=pltpu.VMEM(query.shape, low),
        in_specs=[anywhere] * 7 + [pl.BlockSpec(memory_space=pltpu.SMEM)],
        out_specs=pl.BlockSpec(memory_space=pltpu.VMEM),
        scratch_shapes=[
            pltpu.VMEM((3, span, width), low),
            pltpu.VMEM((2, span, width), low),
            pltpu.VMEM((2, span, width), low),
            pltpu.VMEM((2, heads, span), wide),
            pltpu.VMEM((3, 3, 2, 2, 2, 2, rows, width), low),
            pltpu.VMEM((6, 2, 2, 2, 2, rows, width), wide),
            pltpu.VMEM((6, 2, 2, 2, rows, width), low),
            pltpu.VMEM((6, 2, 2, 2, rows, width), low),
            pltpu.VMEM((6, 2, 2, rows, width), low),
            pltpu.VMEM((6, 2, 2, rows, width), low),
            pltpu.VMEM((6, 2, rows, width), low),
            pltpu.VMEM((6, 2, rows, width), low),
            pltpu.VMEM((3, 2, rows, width), wide),
            pltpu.VMEM((3, 2, rows, width), wide),
            pltpu.VMEM((3, span, width), low),
            pltpu.VMEM((span, hidden), wide),
            pltpu.VMEM((span, hidden), wide),
            pltpu.VMEM((span, hidden), low),
            dma((9,)),
            dma((9,)),
            dma((9,)),
            dma((2, 3, 7)),
            dma((2, 3, 7)),
            dma((3, 15)),
            dma((3, 15)),
            dma((3,)),
            pltpu.VMEM((3, heads, rows, width), low),
            dma((6, 4)),
            dma((6, 4)),
            dma((3,)),
            dma((3,)),
            dma((3,)),
        ],
        compiler_params=pltpu.CompilerParams(
            collective_id=0, has_side_effects=True, vmem_limit_bytes=60 * 1024 * 1024
        ),
    )(query, key, value, jnp.swapaxes(rate, 1, 2), first, third, second, decay)


def solution(mesh):
    placed = (
        P(None, ("groups", "tok"), None),
        P(None, ("groups", "tok"), None),
        P(None, ("groups", "tok"), None),
        P(None, ("groups", "tok"), None),
        P(None, "tok", None),
        P(None, "tok", None),
        P(None, "tok", None),
        P(),
    )
    chips = mesh.shape["tok"] // 2

    def body(*arrays):
        rows = arrays[4].shape[1]
        if rows % 16 or chips != 8 or arrays[4].shape[0] != 2 or mesh.shape["groups"] != 2:
            return shards(*arrays)
        return fused_shards(*arrays)

    return jax.shard_map(
        body,
        mesh=mesh,
        in_specs=placed,
        out_specs=P(None, ("groups", "tok"), None),
        check_vma=False,
    )
```

```python
import jax
import jax.numpy as jnp
from jax import lax
from jax.experimental import pallas as pl
from jax.experimental.pallas import tpu as pltpu
from jax.sharding import PartitionSpec as P

MESH = pl.DeviceIdType.MESH


def forward_parts(weights, inputs):
    first, third, second = weights
    length = inputs.shape[0]
    head_count = first.shape[0]
    shaped = inputs.reshape(length, head_count, -1)
    pre_gate = jnp.einsum("thd,hfd->htf", shaped, first, preferred_element_type=jnp.float32)
    pre_up = jnp.einsum("thd,hfd->htf", shaped, third, preferred_element_type=jnp.float32)
    hidden = (jax.nn.silu(pre_gate) * pre_up).astype(jnp.bfloat16)
    return (shaped, pre_gate, pre_up, hidden)


def apply_block(weights, inputs):
    shaped, pre_gate, pre_up, hidden = forward_parts(weights, inputs)
    result = jnp.einsum("htf,hdf->thd", hidden, weights[2], preferred_element_type=jnp.float32)
    return result.reshape(inputs.shape[0], -1).astype(jnp.bfloat16)


def partial_steps(weights, keys, values, rates):
    shaped, pre_gate, pre_up, hidden = forward_parts(weights, keys)
    length = keys.shape[0]
    head_count = weights[0].shape[0]
    scaled = (
        rates[:, :, None] * values.reshape(length, head_count, -1).astype(jnp.float32)
    ).astype(jnp.bfloat16)
    step_second = jnp.einsum("thd,htf->hdf", scaled, hidden, preferred_element_type=jnp.float32)
    back = jnp.einsum("thd,hdf->htf", scaled, weights[2], preferred_element_type=jnp.float32)
    sig_gate = jax.nn.sigmoid(pre_gate)
    d_gate = (back * pre_up * sig_gate * (1.0 + pre_gate * (1.0 - sig_gate))).astype(jnp.bfloat16)
    d_up = (back * pre_gate * sig_gate).astype(jnp.bfloat16)
    step_first = jnp.einsum("htf,thd->hfd", d_gate, shaped, preferred_element_type=jnp.float32)
    step_third = jnp.einsum("htf,thd->hfd", d_up, shaped, preferred_element_type=jnp.float32)
    return (step_first, step_third, step_second)


def renorm(old, moved):
    old_norm = jnp.sqrt(jnp.sum(old * old, axis=-1, keepdims=True) + 1e-06)
    moved_norm = jnp.sqrt(jnp.sum(moved * moved, axis=-1, keepdims=True) + 1e-06)
    return moved * old_norm / moved_norm


def shards(
    query_tokens,
    key_tokens,
    value_tokens,
    learn_rates,
    fast_first,
    fast_third,
    fast_second,
    momentum_decay,
):
    owned_zero = jnp.stack([fast_first, fast_third, fast_second])
    full_zero = lax.all_gather(owned_zero, "tok", axis=2, tiled=True)
    terms_zero = partial_steps(full_zero, key_tokens[0], value_tokens[0], learn_rates[0])
    terms_one = partial_steps(full_zero, key_tokens[1], value_tokens[1], learn_rates[1])
    step_zero = lax.psum_scatter(
        jnp.stack(terms_zero).astype(jnp.bfloat16), "tok", scatter_dimension=2, tiled=True
    ).astype(jnp.float32)
    step_one = lax.psum_scatter(
        jnp.stack(terms_one).astype(jnp.bfloat16), "tok", scatter_dimension=2, tiled=True
    ).astype(jnp.float32)
    out_zero = apply_block(full_zero, query_tokens[0])
    decay = momentum_decay[None, :, None, None]
    weights_zero = owned_zero.astype(jnp.float32)
    weights_one = renorm(weights_zero, weights_zero + step_zero)
    full_one = lax.all_gather(weights_one.astype(jnp.bfloat16), "tok", axis=2, tiled=True)
    weights_two = renorm(weights_one, weights_one + decay * step_zero + step_one)
    full_two = lax.all_gather(weights_two.astype(jnp.bfloat16), "tok", axis=2, tiled=True)
    out_one = apply_block(full_one, query_tokens[1])
    out_two = apply_block(full_two, query_tokens[2])
    return jnp.stack([out_zero, out_one, out_two])


def dot_nt(a, b):
    return lax.dot_general(a, b, (((1,), (1,)), ((), ())), preferred_element_type=jnp.float32)


def dot_nn(a, b):
    return lax.dot_general(a, b, (((1,), (0,)), ((), ())), preferred_element_type=jnp.float32)


def dot_tn(a, b):
    return lax.dot_general(a, b, (((0,), (0,)), ((), ())), preferred_element_type=jnp.float32)


def kernel(
    query_ref,
    key_ref,
    value_ref,
    rate_ref,
    first_ref,
    third_ref,
    second_ref,
    decay_ref,
    out_ref,
    queries,
    keys,
    values,
    rates,
    full,
    part,
    core_out,
    core_in,
    side_out,
    side_in,
    far_out,
    far_in,
    step_own,
    weight_own,
    result,
    gates,
    ups,
    hiddens,
    swap_send,
    swap_recv,
    local_sem,
    gather_send,
    gather_recv,
    first_send,
    first_recv,
    first_local,
    rows_here,
    sum_send,
    sum_recv,
    side_send,
    side_recv,
    out_send,
    out_recv,
    out_local,
):
    index = lax.axis_index("tok")
    core = index % 2
    lane = (index // 2) % 2
    head = (index // 4) % 2
    pair = index // 8
    group = lax.axis_index("groups")
    across = {"groups": 1 - group}
    partner = {"tok": index + 1 - 2 * core}
    beside = {"tok": index + 2 - 4 * lane}
    mate = {"tok": index + 4 - 8 * head}
    beyond = {"tok": index + 8 - 16 * pair}
    crossed = {"tok": index + 12 - 8 * head - 16 * pair}
    corner = {"groups": 1 - group, "tok": index + 2 - 4 * lane}
    rows = first_ref.shape[1]
    tokens = key_ref.shape[1]
    width = first_ref.shape[2]
    hidden_units = 16 * rows

    for m, ref in enumerate((first_ref, third_ref, second_ref)):
        pltpu.make_async_copy(ref, rows_here.at[m], first_local.at[m]).start()

    barrier = pltpu.get_barrier_semaphore()
    others = (crossed, beyond, corner, mate, beside, across, partner)
    for other in others:
        pl.semaphore_signal(barrier, inc=1, device_id=other, device_id_type=MESH)
    pl.semaphore_wait(barrier, len(others))

    sent = []

    def push(src, dst, send_sem, recv_sem, to):
        return pltpu.make_async_remote_copy(
            src_ref=src,
            dst_ref=dst,
            send_sem=send_sem,
            recv_sem=recv_sem,
            device_id=to,
            device_id_type=MESH,
        )

    def go(copy):
        copy.start()
        sent.append(copy)

    mine = pl.ds(pl.multiple_of(head * width, width), width)
    theirs = pl.ds(pl.multiple_of((1 - head) * width, width), width)
    slot = pl.ds(pl.multiple_of(head * tokens, tokens), tokens)
    other_slot = pl.ds(pl.multiple_of((1 - head) * tokens, tokens), tokens)

    pairs = []
    for b in range(2):
        pairs.append((key_ref.at[b, :, theirs], key_ref.at[b, :, mine], keys.at[b, slot, :]))
        pairs.append((value_ref.at[b, :, theirs], value_ref.at[b, :, mine], values.at[b, slot, :]))
        pairs.append((rate_ref.at[b], rate_ref.at[b], rates.at[b, :, slot]))
    for b in range(3):
        pairs.append((query_ref.at[b, :, theirs], query_ref.at[b, :, mine], queries.at[b, slot, :]))
    swaps = {}
    locals_ = {}

    def swap(first, last):
        for n in range(first, last):
            away, here, target = pairs[n]
            swaps[n] = push(away, target, swap_send.at[n], swap_recv.at[n], mate)
            swaps[n].start()
            locals_[n] = pltpu.make_async_copy(here, target, local_sem.at[n])
            locals_[n].start()

    def ready(n):
        swaps[n].wait_recv()
        locals_[n].wait()

    def block_of(k, m, p, q):
        return full.at[k, m, p, :, q, core]

    def gather_copy(k, m, n, h):
        p, q = (
            (pair, lane),
            (pair, lane),
            (1 - pair, lane),
            (pair, lane),
            (1 - pair, lane),
            (pair, 1 - lane),
            (1 - pair, 1 - lane),
        )[n]
        span = full.at[k, m, p, h, q, core]
        to = (beyond, beside, beside, partner, partner, partner, partner)[n]
        return push(
            span, span, gather_send.at[k - 1, m, n, h], gather_recv.at[k - 1, m, n, h], to
        )

    share = pl.ds(pl.multiple_of(group * (width // 2), width // 2), width // 2)

    def first_copy(m, n):
        ref = rows_here.at[m]
        own = full.at[0, m, pair, head, lane, core]
        near = full.at[0, m, pair, 1 - head, lane, core]
        wide = full.at[0, m, 1 - pair, :, lane, core, :, share]
        src, dst, to = (
            (ref.at[1 - head, :, share], own.at[:, share], mate),
            (ref.at[head, :, share], own.at[:, share], beyond),
            (ref.at[1 - head, :, share], own.at[:, share], crossed),
            (ref.at[head], own, beside),
            (ref.at[head], own, partner),
            (near.at[:, share], near.at[:, share], beside),
            (near.at[:, share], near.at[:, share], across),
            (wide, wide, beside),
            (wide, wide, across),
            (wide, wide, corner),
            (near.at[:, share], near.at[:, share], corner),
            (near, near, partner),
            (block_of(0, m, pair, 1 - lane),) * 2 + (partner,),
            (block_of(0, m, 1 - pair, lane),) * 2 + (partner,),
            (block_of(0, m, 1 - pair, 1 - lane),) * 2 + (partner,),
        )[n]
        return push(src, dst, first_send.at[m, n], first_recv.at[m, n], to)

    def first_here(m):
        return pltpu.make_async_copy(
            rows_here.at[m, head], full.at[0, m, pair, head, lane, core], first_local.at[m]
        )

    def first_start():
        for m, ref in enumerate((first_ref, third_ref, second_ref)):
            pltpu.make_async_copy(ref, rows_here.at[m], first_local.at[m]).wait()
        for m in range(3):
            for n in (2, 1, 0, 3, 4):
                go(first_copy(m, n))
            first_here(m).start()

    def first_spread():
        for m in range(3):
            first_copy(m, 0).wait_recv()
            for n in (5, 10, 6):
                go(first_copy(m, n))
        for m in range(3):
            first_copy(m, 2).wait_recv()
            first_copy(m, 1).wait_recv()
            for n in (7, 9, 8):
                go(first_copy(m, n))
        for m in range(3):
            first_copy(m, 6).wait_recv()
            go(first_copy(m, 11))
            for n in (3, 5, 10):
                first_copy(m, n).wait_recv()
            go(first_copy(m, 12))
        for m in range(3):
            first_copy(m, 8).wait_recv()
            go(first_copy(m, 13))
            first_copy(m, 7).wait_recv()
            first_copy(m, 9).wait_recv()
            go(first_copy(m, 14))

    def first_end(m):
        first_here(m).wait()
        for n in (4, 11, 12, 13, 14):
            first_copy(m, n).wait_recv()

    def gather_own(k, m, h):
        for n in (0, 1, 3):
            go(gather_copy(k, m, n, h))

    def gather_beyond(k, m):
        for h in range(2):
            gather_copy(k, m, 0, h).wait_recv()
            go(gather_copy(k, m, 2, h))
            go(gather_copy(k, m, 4, h))

    def gather_beside(k, m, n):
        for h in range(2):
            gather_copy(k, m, n, h).wait_recv()
            go(gather_copy(k, m, n + 4, h))

    def gather_end(k, m):
        for n in range(3, 7):
            for h in range(2):
                gather_copy(k, m, n, h).wait_recv()

    def core_copy(t):
        return push(
            core_out.at[t], core_in.at[t], sum_send.at[t], sum_recv.at[t], partner
        )

    def side_copy(t, p, n, h):
        return push(
            side_out.at[t, p, h],
            side_in.at[t, p, h],
            side_send.at[t, n, h],
            side_recv.at[t, n, h],
            beside,
        )

    def far_copy(t, h):
        return push(
            far_out.at[t, h], far_in.at[t, h], side_send.at[t, 2, h], side_recv.at[t, 2, h], beyond
        )

    def core_start(t):
        core_out[t] = part[t, :, :, :, 1 - core].astype(jnp.bfloat16)
        go(core_copy(t))

    def core_sum(t, p, q, h):
        return part[t, p, h, q, core] + core_in[t, p, h, q].astype(jnp.float32)

    def side_start(ts):
        for n in (0, 1):
            for t in ts:
                if n == 0:
                    core_copy(t).wait_recv()
                p = 1 - pair if n == 0 else pair
                for h in range(2):
                    side_out[t, p, h] = core_sum(t, p, 1 - lane, h).astype(jnp.bfloat16)
                    go(side_copy(t, p, n, h))

    def far_start(t):
        p = 1 - pair
        for h in range(2):
            side_copy(t, p, 0, h).wait_recv()
            far_out[t, h] = (
                core_sum(t, p, lane, h) + side_in[t, p, h].astype(jnp.float32)
            ).astype(jnp.bfloat16)
            go(far_copy(t, h))

    def total_of(t, h):
        side_copy(t, pair, 1, h).wait_recv()
        near = core_sum(t, pair, lane, h) + side_in[t, pair, h].astype(jnp.float32)
        far_copy(t, h).wait_recv()
        return near + far_in[t, h].astype(jnp.float32)

    order = (2, 0, 1)

    def whole(k, m):
        return full[k, m].reshape(hidden_units, width)

    def forward(k, x):
        gate = dot_nt(x, whole(k, 0))
        up = dot_nt(x, whole(k, 1))
        sig = jax.nn.sigmoid(gate)
        return gate, up, sig, (gate * sig * up).astype(jnp.bfloat16)

    def keys_forward(j):
        gate, up, sig, hidden = forward(0, keys[j])
        gates[...] = gate
        ups[...] = up
        hiddens[...] = hidden

    def steps(j):
        row = jnp.where(head == 0, rates[j, 0:1, :], rates[j, 1:2, :])
        rate = jnp.transpose(jnp.broadcast_to(row, (128, row.shape[1])))[:, 0:1]
        scaled = (rate * values[j].astype(jnp.float32)).astype(jnp.bfloat16)
        part[3 * j + 2] = dot_tn(scaled, hiddens[...]).reshape(part.shape[1:])
        core_start(3 * j + 2)
        if j == 0:
            first_end(2)
        back = dot_nn(scaled, whole(0, 2))
        gate = gates[...]
        sig = jax.nn.sigmoid(gate)
        x = keys[j]
        d_gate = (back * ups[...] * sig * (1.0 + gate * (1.0 - sig))).astype(jnp.bfloat16)
        part[3 * j] = dot_tn(d_gate, x).reshape(part.shape[1:])
        core_start(3 * j)
        d_up = (back * gate * sig).astype(jnp.bfloat16)
        part[3 * j + 1] = dot_tn(d_up, x).reshape(part.shape[1:])
        core_start(3 * j + 1)

    outs = []

    def read_hidden(k):
        gate, up, sig, hidden = forward(k, queries[k])
        hiddens[...] = hidden

    def read_out(k):
        result[k] = dot_nt(hiddens[...], whole(k, 2)).astype(jnp.bfloat16)
        send_out(k)
        keep_out(k)

    def send_out(k):
        away = push(
            result.at[k, other_slot, :],
            out_ref.at[k, :, mine],
            out_send.at[k],
            out_recv.at[k],
            mate,
        )
        away.start()
        outs.append(away)

    def keep_out(k):
        here = pltpu.make_async_copy(
            result.at[k, slot, :], out_ref.at[k, :, mine], out_local.at[k]
        )
        here.start()
        outs.append(here)

    first_start()
    swap(0, 6)
    first_spread()
    for m in range(2):
        first_end(m)
    for n in range(0, 3):
        ready(n)
    keys_forward(0)
    steps(0)
    side_start(order)
    for n in range(3, 6):
        ready(n)
    keys_forward(1)
    steps(1)
    for m in order:
        far_start(m)
        side_start([3 + m])
    swap(6, 7)
    for m in order:
        for h in range(2):
            moment = total_of(m, h)
            step_own[m, h] = moment
            old = full[0, m, pair, h, lane, core].astype(jnp.float32)
            fresh = renorm(old, old + moment)
            weight_own[m, h] = fresh
            full[1, m, pair, h, lane, core] = fresh.astype(jnp.bfloat16)
            gather_own(1, m, h)
    decay = decay_ref[head]
    for m in order:
        far_start(3 + m)
    swap(7, 8)
    for m in order:
        gather_beyond(1, m)
        gather_beside(1, m, 1)
    ready(6)
    read_hidden(0)
    read_out(0)
    for m in order:
        for h in range(2):
            moment = decay * step_own[m, h] + total_of(3 + m, h)
            old = weight_own[m, h]
            fresh = renorm(old, old + moment)
            full[2, m, pair, h, lane, core] = fresh.astype(jnp.bfloat16)
            gather_own(2, m, h)
    swap(8, 9)
    for m in order:
        gather_beside(1, m, 2)
    for m in order:
        gather_beyond(2, m)
        gather_beside(2, m, 1)
    for m in range(3):
        gather_end(1, m)
    ready(7)
    read_hidden(1)
    read_out(1)
    ready(8)
    for m in order:
        gather_beside(2, m, 2)
    gather_end(2, 2)
    gather_end(2, 0)
    gates[...] = dot_nt(queries[2], whole(2, 0))
    gather_end(2, 1)
    for place in (other_slot, slot):
        gate = gates[place, :]
        up = dot_nt(queries[2, place, :], whole(2, 1))
        hidden = (gate * jax.nn.sigmoid(gate) * up).astype(jnp.bfloat16)
        result[2, place, :] = dot_nt(hidden, whole(2, 2)).astype(jnp.bfloat16)
        if place is other_slot:
            send_out(2)
    keep_out(2)

    for n in range(len(pairs)):
        swaps[n].wait_send()
    for copy in sent:
        copy.wait_send()
    for copy in outs:
        copy.wait()


def fused_shards(query, key, value, rate, first, third, second, decay):
    blocks, tokens, features = query.shape
    heads, rows, width = first.shape
    hidden = 16 * rows
    span = 2 * tokens
    anywhere = pl.BlockSpec(memory_space=pl.ANY)
    dma = pltpu.SemaphoreType.DMA
    low, wide = jnp.bfloat16, jnp.float32
    return pl.pallas_call(
        kernel,
        out_shape=pltpu.VMEM(query.shape, low),
        in_specs=[anywhere] * 7 + [pl.BlockSpec(memory_space=pltpu.SMEM)],
        out_specs=pl.BlockSpec(memory_space=pltpu.VMEM),
        scratch_shapes=[
            pltpu.VMEM((3, span, width), low),
            pltpu.VMEM((2, span, width), low),
            pltpu.VMEM((2, span, width), low),
            pltpu.VMEM((2, heads, span), wide),
            pltpu.VMEM((3, 3, 2, 2, 2, 2, rows, width), low),
            pltpu.VMEM((6, 2, 2, 2, 2, rows, width), wide),
            pltpu.VMEM((6, 2, 2, 2, rows, width), low),
            pltpu.VMEM((6, 2, 2, 2, rows, width), low),
            pltpu.VMEM((6, 2, 2, rows, width), low),
            pltpu.VMEM((6, 2, 2, rows, width), low),
            pltpu.VMEM((6, 2, rows, width), low),
            pltpu.VMEM((6, 2, rows, width), low),
            pltpu.VMEM((3, 2, rows, width), wide),
            pltpu.VMEM((3, 2, rows, width), wide),
            pltpu.VMEM((3, span, width), low),
            pltpu.VMEM((span, hidden), wide),
            pltpu.VMEM((span, hidden), wide),
            pltpu.VMEM((span, hidden), low),
            dma((9,)),
            dma((9,)),
            dma((9,)),
            dma((2, 3, 7, 2)),
            dma((2, 3, 7, 2)),
            dma((3, 15)),
            dma((3, 15)),
            dma((3,)),
            pltpu.VMEM((3, heads, rows, width), low),
            dma((6,)),
            dma((6,)),
            dma((6, 3, 2)),
            dma((6, 3, 2)),
            dma((3,)),
            dma((3,)),
            dma((3,)),
        ],
        compiler_params=pltpu.CompilerParams(
            collective_id=0, has_side_effects=True, vmem_limit_bytes=60 * 1024 * 1024
        ),
    )(query, key, value, jnp.swapaxes(rate, 1, 2), first, third, second, decay)


def solution(mesh):
    placed = (
        P(None, ("groups", "tok"), None),
        P(None, ("groups", "tok"), None),
        P(None, ("groups", "tok"), None),
        P(None, ("groups", "tok"), None),
        P(None, "tok", None),
        P(None, "tok", None),
        P(None, "tok", None),
        P(),
    )
    chips = mesh.shape["tok"] // 2

    def body(*arrays):
        rows = arrays[4].shape[1]
        if rows % 16 or chips != 8 or arrays[4].shape[0] != 2 or mesh.shape["groups"] != 2:
            return shards(*arrays)
        return fused_shards(*arrays)

    return jax.shard_map(
        body,
        mesh=mesh,
        in_specs=placed,
        out_specs=P(None, ("groups", "tok"), None),
        check_vma=False,
    )
```

```python
import jax
import jax.numpy as jnp
from jax import lax
from jax.experimental import pallas as pl
from jax.experimental.pallas import tpu as pltpu
from jax.sharding import PartitionSpec as P

MESH = pl.DeviceIdType.MESH


def forward_parts(weights, inputs):
    first, third, second = weights
    length = inputs.shape[0]
    head_count = first.shape[0]
    shaped = inputs.reshape(length, head_count, -1)
    pre_gate = jnp.einsum("thd,hfd->htf", shaped, first, preferred_element_type=jnp.float32)
    pre_up = jnp.einsum("thd,hfd->htf", shaped, third, preferred_element_type=jnp.float32)
    hidden = (jax.nn.silu(pre_gate) * pre_up).astype(jnp.bfloat16)
    return (shaped, pre_gate, pre_up, hidden)


def apply_block(weights, inputs):
    shaped, pre_gate, pre_up, hidden = forward_parts(weights, inputs)
    result = jnp.einsum("htf,hdf->thd", hidden, weights[2], preferred_element_type=jnp.float32)
    return result.reshape(inputs.shape[0], -1).astype(jnp.bfloat16)


def partial_steps(weights, keys, values, rates):
    shaped, pre_gate, pre_up, hidden = forward_parts(weights, keys)
    length = keys.shape[0]
    head_count = weights[0].shape[0]
    scaled = (
        rates[:, :, None] * values.reshape(length, head_count, -1).astype(jnp.float32)
    ).astype(jnp.bfloat16)
    step_second = jnp.einsum("thd,htf->hdf", scaled, hidden, preferred_element_type=jnp.float32)
    back = jnp.einsum("thd,hdf->htf", scaled, weights[2], preferred_element_type=jnp.float32)
    sig_gate = jax.nn.sigmoid(pre_gate)
    d_gate = (back * pre_up * sig_gate * (1.0 + pre_gate * (1.0 - sig_gate))).astype(jnp.bfloat16)
    d_up = (back * pre_gate * sig_gate).astype(jnp.bfloat16)
    step_first = jnp.einsum("htf,thd->hfd", d_gate, shaped, preferred_element_type=jnp.float32)
    step_third = jnp.einsum("htf,thd->hfd", d_up, shaped, preferred_element_type=jnp.float32)
    return (step_first, step_third, step_second)


def renorm(old, moved):
    old_norm = jnp.sqrt(jnp.sum(old * old, axis=-1, keepdims=True) + 1e-06)
    moved_norm = jnp.sqrt(jnp.sum(moved * moved, axis=-1, keepdims=True) + 1e-06)
    return moved * old_norm / moved_norm


def shards(
    query_tokens,
    key_tokens,
    value_tokens,
    learn_rates,
    fast_first,
    fast_third,
    fast_second,
    momentum_decay,
):
    owned_zero = jnp.stack([fast_first, fast_third, fast_second])
    full_zero = lax.all_gather(owned_zero, "tok", axis=2, tiled=True)
    terms_zero = partial_steps(full_zero, key_tokens[0], value_tokens[0], learn_rates[0])
    terms_one = partial_steps(full_zero, key_tokens[1], value_tokens[1], learn_rates[1])
    step_zero = lax.psum_scatter(
        jnp.stack(terms_zero).astype(jnp.bfloat16), "tok", scatter_dimension=2, tiled=True
    ).astype(jnp.float32)
    step_one = lax.psum_scatter(
        jnp.stack(terms_one).astype(jnp.bfloat16), "tok", scatter_dimension=2, tiled=True
    ).astype(jnp.float32)
    out_zero = apply_block(full_zero, query_tokens[0])
    decay = momentum_decay[None, :, None, None]
    weights_zero = owned_zero.astype(jnp.float32)
    weights_one = renorm(weights_zero, weights_zero + step_zero)
    full_one = lax.all_gather(weights_one.astype(jnp.bfloat16), "tok", axis=2, tiled=True)
    weights_two = renorm(weights_one, weights_one + decay * step_zero + step_one)
    full_two = lax.all_gather(weights_two.astype(jnp.bfloat16), "tok", axis=2, tiled=True)
    out_one = apply_block(full_one, query_tokens[1])
    out_two = apply_block(full_two, query_tokens[2])
    return jnp.stack([out_zero, out_one, out_two])


def dot_nt(a, b):
    return lax.dot_general(a, b, (((1,), (1,)), ((), ())), preferred_element_type=jnp.float32)


def dot_nn(a, b):
    return lax.dot_general(a, b, (((1,), (0,)), ((), ())), preferred_element_type=jnp.float32)


def dot_tn(a, b):
    return lax.dot_general(a, b, (((0,), (0,)), ((), ())), preferred_element_type=jnp.float32)


def kernel(
    query_ref,
    key_ref,
    value_ref,
    rate_ref,
    first_ref,
    third_ref,
    second_ref,
    decay_ref,
    out_ref,
    queries,
    keys,
    values,
    rates,
    full,
    part,
    core_out,
    core_in,
    side_out,
    side_in,
    far_out,
    far_in,
    step_own,
    weight_own,
    result,
    gates,
    ups,
    hiddens,
    swap_send,
    swap_recv,
    local_sem,
    gather_send,
    gather_recv,
    first_send,
    first_recv,
    first_local,
    rows_here,
    sum_send,
    sum_recv,
    side_send,
    side_recv,
    out_send,
    out_recv,
    out_local,
):
    index = lax.axis_index("tok")
    core = index % 2
    lane = (index // 2) % 2
    head = (index // 4) % 2
    pair = index // 8
    group = lax.axis_index("groups")
    across = {"groups": 1 - group}
    partner = {"tok": index + 1 - 2 * core}
    beside = {"tok": index + 2 - 4 * lane}
    mate = {"tok": index + 4 - 8 * head}
    beyond = {"tok": index + 8 - 16 * pair}
    crossed = {"tok": index + 12 - 8 * head - 16 * pair}
    corner = {"groups": 1 - group, "tok": index + 2 - 4 * lane}
    rows = first_ref.shape[1]
    tokens = key_ref.shape[1]
    width = first_ref.shape[2]
    hidden_units = 16 * rows

    for m, ref in enumerate((first_ref, third_ref, second_ref)):
        pltpu.make_async_copy(ref, rows_here.at[m], first_local.at[m]).start()

    barrier = pltpu.get_barrier_semaphore()
    others = (crossed, beyond, corner, mate, beside, across, partner)
    for other in others:
        pl.semaphore_signal(barrier, inc=1, device_id=other, device_id_type=MESH)
    pl.semaphore_wait(barrier, len(others))

    sent = []

    def push(src, dst, send_sem, recv_sem, to):
        return pltpu.make_async_remote_copy(
            src_ref=src,
            dst_ref=dst,
            send_sem=send_sem,
            recv_sem=recv_sem,
            device_id=to,
            device_id_type=MESH,
        )

    def go(copy):
        copy.start()
        sent.append(copy)

    mine = pl.ds(pl.multiple_of(head * width, width), width)
    theirs = pl.ds(pl.multiple_of((1 - head) * width, width), width)
    slot = pl.ds(pl.multiple_of(head * tokens, tokens), tokens)
    other_slot = pl.ds(pl.multiple_of((1 - head) * tokens, tokens), tokens)

    pairs = []
    for b in range(2):
        pairs.append((key_ref.at[b, :, theirs], key_ref.at[b, :, mine], keys.at[b, slot, :]))
        pairs.append((value_ref.at[b, :, theirs], value_ref.at[b, :, mine], values.at[b, slot, :]))
        pairs.append((rate_ref.at[b], rate_ref.at[b], rates.at[b, :, slot]))
    for b in range(3):
        pairs.append((query_ref.at[b, :, theirs], query_ref.at[b, :, mine], queries.at[b, slot, :]))
    swaps = {}
    locals_ = {}

    def swap(first, last):
        for n in range(first, last):
            away, here, target = pairs[n]
            swaps[n] = push(away, target, swap_send.at[n], swap_recv.at[n], mate)
            swaps[n].start()
            locals_[n] = pltpu.make_async_copy(here, target, local_sem.at[n])
            locals_[n].start()

    def ready(n):
        swaps[n].wait_recv()
        locals_[n].wait()

    def block_of(k, m, p, q):
        return full.at[k, m, p, :, q, core]

    def gather_copy(k, m, n, h):
        p, q = (
            (pair, lane),
            (pair, lane),
            (1 - pair, lane),
            (pair, lane),
            (1 - pair, lane),
            (pair, 1 - lane),
            (1 - pair, 1 - lane),
        )[n]
        span = full.at[k, m, p, h, q, core]
        to = (beyond, beside, beside, partner, partner, partner, partner)[n]
        return push(
            span, span, gather_send.at[k - 1, m, n, h], gather_recv.at[k - 1, m, n, h], to
        )

    share = pl.ds(pl.multiple_of(group * (width // 2), width // 2), width // 2)

    def first_copy(m, n):
        ref = rows_here.at[m]
        own = full.at[0, m, pair, head, lane, core]
        near = full.at[0, m, pair, 1 - head, lane, core]
        wide = full.at[0, m, 1 - pair, :, lane, core, :, share]
        src, dst, to = (
            (ref.at[1 - head, :, share], own.at[:, share], mate),
            (ref.at[head, :, share], own.at[:, share], beyond),
            (ref.at[1 - head, :, share], own.at[:, share], crossed),
            (ref.at[head], own, beside),
            (ref.at[head], own, partner),
            (near.at[:, share], near.at[:, share], beside),
            (near.at[:, share], near.at[:, share], across),
            (wide, wide, beside),
            (wide, wide, across),
            (wide, wide, corner),
            (near.at[:, share], near.at[:, share], corner),
            (near, near, partner),
            (block_of(0, m, pair, 1 - lane),) * 2 + (partner,),
            (block_of(0, m, 1 - pair, lane),) * 2 + (partner,),
            (block_of(0, m, 1 - pair, 1 - lane),) * 2 + (partner,),
        )[n]
        return push(src, dst, first_send.at[m, n], first_recv.at[m, n], to)

    def first_here(m):
        return pltpu.make_async_copy(
            rows_here.at[m, head], full.at[0, m, pair, head, lane, core], first_local.at[m]
        )

    def first_start():
        for m, ref in enumerate((first_ref, third_ref, second_ref)):
            pltpu.make_async_copy(ref, rows_here.at[m], first_local.at[m]).wait()
        for m in range(3):
            for n in (2, 1, 0, 3, 4):
                go(first_copy(m, n))
            first_here(m).start()

    def first_spread():
        for m in range(3):
            first_copy(m, 0).wait_recv()
            for n in (5, 10, 6):
                go(first_copy(m, n))
        for m in range(3):
            first_copy(m, 2).wait_recv()
            first_copy(m, 1).wait_recv()
            for n in (7, 9, 8):
                go(first_copy(m, n))
        swap(3, 6)
        for m in range(3):
            first_copy(m, 6).wait_recv()
            go(first_copy(m, 11))
            for n in (3, 5, 10):
                first_copy(m, n).wait_recv()
            go(first_copy(m, 12))
        for m in range(3):
            first_copy(m, 8).wait_recv()
            go(first_copy(m, 13))
            first_copy(m, 7).wait_recv()
            first_copy(m, 9).wait_recv()
            go(first_copy(m, 14))

    def first_end(m):
        first_here(m).wait()
        for n in (4, 11, 12, 13, 14):
            first_copy(m, n).wait_recv()

    def gather_own(k, m, h):
        for n in (0, 1, 3):
            go(gather_copy(k, m, n, h))

    def gather_beyond(k, m):
        for h in range(2):
            gather_copy(k, m, 0, h).wait_recv()
            go(gather_copy(k, m, 2, h))
            go(gather_copy(k, m, 4, h))

    def gather_beside(k, m, n):
        for h in range(2):
            gather_copy(k, m, n, h).wait_recv()
            go(gather_copy(k, m, n + 4, h))

    def gather_end(k, m):
        for n in range(3, 7):
            for h in range(2):
                gather_copy(k, m, n, h).wait_recv()

    def core_copy(t):
        return push(
            core_out.at[t], core_in.at[t], sum_send.at[t], sum_recv.at[t], partner
        )

    def side_copy(t, p, n, h):
        return push(
            side_out.at[t, p, h],
            side_in.at[t, p, h],
            side_send.at[t, n, h],
            side_recv.at[t, n, h],
            beside,
        )

    def far_copy(t, h):
        return push(
            far_out.at[t, h], far_in.at[t, h], side_send.at[t, 2, h], side_recv.at[t, 2, h], beyond
        )

    def core_start(t):
        core_out[t] = part[t, :, :, :, 1 - core].astype(jnp.bfloat16)
        go(core_copy(t))

    def core_sum(t, p, q, h):
        return part[t, p, h, q, core] + core_in[t, p, h, q].astype(jnp.float32)

    def side_piece(t, n):
        if n == 0:
            core_copy(t).wait_recv()
        p = 1 - pair if n == 0 else pair
        for h in range(2):
            side_out[t, p, h] = core_sum(t, p, 1 - lane, h).astype(jnp.bfloat16)
            go(side_copy(t, p, n, h))

    def side_start(ts):
        for n in (0, 1):
            for t in ts:
                side_piece(t, n)

    def far_start(t):
        p = 1 - pair
        for h in range(2):
            side_copy(t, p, 0, h).wait_recv()
            far_out[t, h] = (
                core_sum(t, p, lane, h) + side_in[t, p, h].astype(jnp.float32)
            ).astype(jnp.bfloat16)
            go(far_copy(t, h))

    def total_of(t, h):
        side_copy(t, pair, 1, h).wait_recv()
        near = core_sum(t, pair, lane, h) + side_in[t, pair, h].astype(jnp.float32)
        far_copy(t, h).wait_recv()
        return near + far_in[t, h].astype(jnp.float32)

    order = (2, 0, 1)

    def whole(k, m):
        return full[k, m].reshape(hidden_units, width)

    def forward(k, x):
        gate = dot_nt(x, whole(k, 0))
        up = dot_nt(x, whole(k, 1))
        sig = jax.nn.sigmoid(gate)
        return gate, up, sig, (gate * sig * up).astype(jnp.bfloat16)

    def keys_forward(j):
        gate, up, sig, hidden = forward(0, keys[j])
        gates[...] = gate
        ups[...] = up
        hiddens[...] = hidden

    def steps(j):
        row = jnp.where(head == 0, rates[j, 0:1, :], rates[j, 1:2, :])
        rate = jnp.transpose(jnp.broadcast_to(row, (128, row.shape[1])))[:, 0:1]
        scaled = (rate * values[j].astype(jnp.float32)).astype(jnp.bfloat16)
        part[3 * j + 2] = dot_tn(scaled, hiddens[...]).reshape(part.shape[1:])
        core_start(3 * j + 2)
        if j == 0:
            first_end(2)
        back = dot_nn(scaled, whole(0, 2))
        gate = gates[...]
        sig = jax.nn.sigmoid(gate)
        x = keys[j]
        d_gate = (back * ups[...] * sig * (1.0 + gate * (1.0 - sig))).astype(jnp.bfloat16)
        part[3 * j] = dot_tn(d_gate, x).reshape(part.shape[1:])
        core_start(3 * j)
        d_up = (back * gate * sig).astype(jnp.bfloat16)
        part[3 * j + 1] = dot_tn(d_up, x).reshape(part.shape[1:])
        core_start(3 * j + 1)

    outs = []

    def read_hidden(k):
        gate, up, sig, hidden = forward(k, queries[k])
        hiddens[...] = hidden

    def read_out(k):
        result[k] = dot_nt(hiddens[...], whole(k, 2)).astype(jnp.bfloat16)
        send_out(k)
        keep_out(k)

    def send_out(k):
        away = push(
            result.at[k, other_slot, :],
            out_ref.at[k, :, mine],
            out_send.at[k],
            out_recv.at[k],
            mate,
        )
        away.start()
        outs.append(away)

    def keep_out(k):
        here = pltpu.make_async_copy(
            result.at[k, slot, :], out_ref.at[k, :, mine], out_local.at[k]
        )
        here.start()
        outs.append(here)

    first_start()
    swap(0, 3)
    first_spread()
    for m in range(2):
        first_end(m)
    for n in range(0, 3):
        ready(n)
    keys_forward(0)
    steps(0)
    side_start(order)
    for m in order:
        far_start(m)
    for n in range(3, 6):
        ready(n)
    keys_forward(1)
    steps(1)
    for m in order:
        side_piece(3 + m, 0)
    for m in order:
        side_piece(3 + m, 1)
    swap(6, 7)
    for m in order:
        for h in range(2):
            moment = total_of(m, h)
            step_own[m, h] = moment
            old = full[0, m, pair, h, lane, core].astype(jnp.float32)
            fresh = renorm(old, old + moment)
            weight_own[m, h] = fresh
            full[1, m, pair, h, lane, core] = fresh.astype(jnp.bfloat16)
            gather_own(1, m, h)
    decay = decay_ref[head]
    last = (0, 1, 2)
    for m in last:
        far_start(3 + m)
    swap(7, 8)
    for m in order:
        gather_beyond(1, m)
        gather_beside(1, m, 1)
    ready(6)
    read_hidden(0)
    read_out(0)
    for m in last:
        for h in range(2):
            moment = decay * step_own[m, h] + total_of(3 + m, h)
            old = weight_own[m, h]
            fresh = renorm(old, old + moment)
            full[2, m, pair, h, lane, core] = fresh.astype(jnp.bfloat16)
            gather_own(2, m, h)
    swap(8, 9)
    for m in order:
        gather_beside(1, m, 2)
    for m in last:
        gather_beyond(2, m)
        gather_beside(2, m, 1)
    for m in range(3):
        gather_end(1, m)
    ready(7)
    read_hidden(1)
    read_out(1)
    ready(8)
    for m in range(2):
        gather_beside(2, m, 2)
    for m in range(2):
        gather_end(2, m)
    gate, up, sig, hidden = forward(2, queries[2])
    hiddens[...] = hidden
    for n in (3, 5):
        for h in range(2):
            gather_copy(2, 2, n, h).wait_recv()
    columns = width // 2
    for n, p in enumerate((pair, 1 - pair)):
        if n == 1:
            gather_beside(2, 2, 2)
            for e in (4, 6):
                for h in range(2):
                    gather_copy(2, 2, e, h).wait_recv()
        some = pl.ds(pl.multiple_of(p * columns, columns), columns)
        down = full[2, 2, p].reshape(columns, width)
        result[2, :, some] = dot_nt(hiddens[...], down).astype(jnp.bfloat16)
        place = pl.ds(pl.multiple_of(head * width + p * columns, columns), columns)
        away = push(
            result.at[2, other_slot, some],
            out_ref.at[2, :, place],
            out_send.at[2 + n],
            out_recv.at[2 + n],
            mate,
        )
        away.start()
        outs.append(away)
    keep_out(2)

    for n in range(len(pairs)):
        swaps[n].wait_send()
    for copy in sent:
        copy.wait_send()
    for copy in outs:
        copy.wait()


def fused_shards(query, key, value, rate, first, third, second, decay):
    blocks, tokens, features = query.shape
    heads, rows, width = first.shape
    hidden = 16 * rows
    span = 2 * tokens
    anywhere = pl.BlockSpec(memory_space=pl.ANY)
    dma = pltpu.SemaphoreType.DMA
    low, wide = jnp.bfloat16, jnp.float32
    return pl.pallas_call(
        kernel,
        out_shape=pltpu.VMEM(query.shape, low),
        in_specs=[anywhere] * 7 + [pl.BlockSpec(memory_space=pltpu.SMEM)],
        out_specs=pl.BlockSpec(memory_space=pltpu.VMEM),
        scratch_shapes=[
            pltpu.VMEM((3, span, width), low),
            pltpu.VMEM((2, span, width), low),
            pltpu.VMEM((2, span, width), low),
            pltpu.VMEM((2, heads, span), wide),
            pltpu.VMEM((3, 3, 2, 2, 2, 2, rows, width), low),
            pltpu.VMEM((6, 2, 2, 2, 2, rows, width), wide),
            pltpu.VMEM((6, 2, 2, 2, rows, width), low),
            pltpu.VMEM((6, 2, 2, 2, rows, width), low),
            pltpu.VMEM((6, 2, 2, rows, width), low),
            pltpu.VMEM((6, 2, 2, rows, width), low),
            pltpu.VMEM((6, 2, rows, width), low),
            pltpu.VMEM((6, 2, rows, width), low),
            pltpu.VMEM((3, 2, rows, width), wide),
            pltpu.VMEM((3, 2, rows, width), wide),
            pltpu.VMEM((3, span, width), low),
            pltpu.VMEM((span, hidden), wide),
            pltpu.VMEM((span, hidden), wide),
            pltpu.VMEM((span, hidden), low),
            dma((9,)),
            dma((9,)),
            dma((9,)),
            dma((2, 3, 7, 2)),
            dma((2, 3, 7, 2)),
            dma((3, 15)),
            dma((3, 15)),
            dma((3,)),
            pltpu.VMEM((3, heads, rows, width), low),
            dma((6,)),
            dma((6,)),
            dma((6, 3, 2)),
            dma((6, 3, 2)),
            dma((4,)),
            dma((4,)),
            dma((3,)),
        ],
        compiler_params=pltpu.CompilerParams(
            collective_id=0, has_side_effects=True, vmem_limit_bytes=60 * 1024 * 1024
        ),
    )(query, key, value, jnp.swapaxes(rate, 1, 2), first, third, second, decay)


def solution(mesh):
    placed = (
        P(None, ("groups", "tok"), None),
        P(None, ("groups", "tok"), None),
        P(None, ("groups", "tok"), None),
        P(None, ("groups", "tok"), None),
        P(None, "tok", None),
        P(None, "tok", None),
        P(None, "tok", None),
        P(),
    )
    chips = mesh.shape["tok"] // 2

    def body(*arrays):
        rows = arrays[4].shape[1]
        if rows % 16 or chips != 8 or arrays[4].shape[0] != 2 or mesh.shape["groups"] != 2:
            return shards(*arrays)
        return fused_shards(*arrays)

    return jax.shard_map(
        body,
        mesh=mesh,
        in_specs=placed,
        out_specs=P(None, ("groups", "tok"), None),
        check_vma=False,
    )
```

```python
import jax
import jax.numpy as jnp
from jax import lax
from jax.experimental import pallas as pl
from jax.experimental.pallas import tpu as pltpu
from jax.sharding import PartitionSpec as P

MESH = pl.DeviceIdType.MESH


def forward_parts(weights, inputs):
    first, third, second = weights
    length = inputs.shape[0]
    head_count = first.shape[0]
    shaped = inputs.reshape(length, head_count, -1)
    pre_gate = jnp.einsum("thd,hfd->htf", shaped, first, preferred_element_type=jnp.float32)
    pre_up = jnp.einsum("thd,hfd->htf", shaped, third, preferred_element_type=jnp.float32)
    hidden = (jax.nn.silu(pre_gate) * pre_up).astype(jnp.bfloat16)
    return (shaped, pre_gate, pre_up, hidden)


def apply_block(weights, inputs):
    shaped, pre_gate, pre_up, hidden = forward_parts(weights, inputs)
    result = jnp.einsum("htf,hdf->thd", hidden, weights[2], preferred_element_type=jnp.float32)
    return result.reshape(inputs.shape[0], -1).astype(jnp.bfloat16)


def partial_steps(weights, keys, values, rates):
    shaped, pre_gate, pre_up, hidden = forward_parts(weights, keys)
    length = keys.shape[0]
    head_count = weights[0].shape[0]
    scaled = (
        rates[:, :, None] * values.reshape(length, head_count, -1).astype(jnp.float32)
    ).astype(jnp.bfloat16)
    step_second = jnp.einsum("thd,htf->hdf", scaled, hidden, preferred_element_type=jnp.float32)
    back = jnp.einsum("thd,hdf->htf", scaled, weights[2], preferred_element_type=jnp.float32)
    sig_gate = jax.nn.sigmoid(pre_gate)
    d_gate = (back * pre_up * sig_gate * (1.0 + pre_gate * (1.0 - sig_gate))).astype(jnp.bfloat16)
    d_up = (back * pre_gate * sig_gate).astype(jnp.bfloat16)
    step_first = jnp.einsum("htf,thd->hfd", d_gate, shaped, preferred_element_type=jnp.float32)
    step_third = jnp.einsum("htf,thd->hfd", d_up, shaped, preferred_element_type=jnp.float32)
    return (step_first, step_third, step_second)


def renorm(old, moved):
    old_norm = jnp.sqrt(jnp.sum(old * old, axis=-1, keepdims=True) + 1e-06)
    moved_norm = jnp.sqrt(jnp.sum(moved * moved, axis=-1, keepdims=True) + 1e-06)
    return moved * old_norm / moved_norm


def shards(
    query_tokens,
    key_tokens,
    value_tokens,
    learn_rates,
    fast_first,
    fast_third,
    fast_second,
    momentum_decay,
):
    owned_zero = jnp.stack([fast_first, fast_third, fast_second])
    full_zero = lax.all_gather(owned_zero, "tok", axis=2, tiled=True)
    terms_zero = partial_steps(full_zero, key_tokens[0], value_tokens[0], learn_rates[0])
    terms_one = partial_steps(full_zero, key_tokens[1], value_tokens[1], learn_rates[1])
    step_zero = lax.psum_scatter(
        jnp.stack(terms_zero).astype(jnp.bfloat16), "tok", scatter_dimension=2, tiled=True
    ).astype(jnp.float32)
    step_one = lax.psum_scatter(
        jnp.stack(terms_one).astype(jnp.bfloat16), "tok", scatter_dimension=2, tiled=True
    ).astype(jnp.float32)
    out_zero = apply_block(full_zero, query_tokens[0])
    decay = momentum_decay[None, :, None, None]
    weights_zero = owned_zero.astype(jnp.float32)
    weights_one = renorm(weights_zero, weights_zero + step_zero)
    full_one = lax.all_gather(weights_one.astype(jnp.bfloat16), "tok", axis=2, tiled=True)
    weights_two = renorm(weights_one, weights_one + decay * step_zero + step_one)
    full_two = lax.all_gather(weights_two.astype(jnp.bfloat16), "tok", axis=2, tiled=True)
    out_one = apply_block(full_one, query_tokens[1])
    out_two = apply_block(full_two, query_tokens[2])
    return jnp.stack([out_zero, out_one, out_two])


def dot_nt(a, b):
    return lax.dot_general(a, b, (((1,), (1,)), ((), ())), preferred_element_type=jnp.float32)


def dot_nn(a, b):
    return lax.dot_general(a, b, (((1,), (0,)), ((), ())), preferred_element_type=jnp.float32)


def dot_tn(a, b):
    return lax.dot_general(a, b, (((0,), (0,)), ((), ())), preferred_element_type=jnp.float32)


def kernel(
    query_ref,
    key_ref,
    value_ref,
    rate_ref,
    first_ref,
    third_ref,
    second_ref,
    decay_ref,
    out_ref,
    queries,
    keys,
    values,
    rates,
    full,
    part,
    core_out,
    core_in,
    side_out,
    side_in,
    far_out,
    far_in,
    step_own,
    weight_own,
    result,
    gates,
    ups,
    hiddens,
    swap_send,
    swap_recv,
    local_sem,
    gather_send,
    gather_recv,
    first_send,
    first_recv,
    first_local,
    rows_here,
    sum_send,
    sum_recv,
    side_send,
    side_recv,
    out_send,
    out_recv,
    out_local,
):
    index = lax.axis_index("tok")
    core = index % 2
    lane = (index // 2) % 2
    head = (index // 4) % 2
    pair = index // 8
    group = lax.axis_index("groups")
    across = {"groups": 1 - group}
    partner = {"tok": index + 1 - 2 * core}
    beside = {"tok": index + 2 - 4 * lane}
    mate = {"tok": index + 4 - 8 * head}
    beyond = {"tok": index + 8 - 16 * pair}
    crossed = {"tok": index + 12 - 8 * head - 16 * pair}
    corner = {"groups": 1 - group, "tok": index + 2 - 4 * lane}
    rows = first_ref.shape[1]
    tokens = key_ref.shape[1]
    width = first_ref.shape[2]
    hidden_units = 16 * rows

    for m, ref in enumerate((first_ref, third_ref, second_ref)):
        pltpu.make_async_copy(ref, rows_here.at[m], first_local.at[m]).start()

    barrier = pltpu.get_barrier_semaphore()
    others = (crossed, beyond, corner, mate, beside, across, partner)
    for other in others:
        pl.semaphore_signal(barrier, inc=1, device_id=other, device_id_type=MESH)
    pl.semaphore_wait(barrier, len(others))

    sent = []

    def push(src, dst, send_sem, recv_sem, to):
        return pltpu.make_async_remote_copy(
            src_ref=src,
            dst_ref=dst,
            send_sem=send_sem,
            recv_sem=recv_sem,
            device_id=to,
            device_id_type=MESH,
        )

    def go(copy):
        copy.start()
        sent.append(copy)

    mine = pl.ds(pl.multiple_of(head * width, width), width)
    theirs = pl.ds(pl.multiple_of((1 - head) * width, width), width)
    slot = pl.ds(pl.multiple_of(head * tokens, tokens), tokens)
    other_slot = pl.ds(pl.multiple_of((1 - head) * tokens, tokens), tokens)

    pairs = []
    for b in range(2):
        pairs.append((key_ref.at[b, :, theirs], key_ref.at[b, :, mine], keys.at[b, slot, :]))
        pairs.append((value_ref.at[b, :, theirs], value_ref.at[b, :, mine], values.at[b, slot, :]))
        pairs.append((rate_ref.at[b], rate_ref.at[b], rates.at[b, :, slot]))
    for b in range(3):
        pairs.append((query_ref.at[b, :, theirs], query_ref.at[b, :, mine], queries.at[b, slot, :]))
    swaps = {}
    locals_ = {}

    def swap(first, last):
        for n in range(first, last):
            away, here, target = pairs[n]
            swaps[n] = push(away, target, swap_send.at[n], swap_recv.at[n], mate)
            swaps[n].start()
            locals_[n] = pltpu.make_async_copy(here, target, local_sem.at[n])
            locals_[n].start()

    def ready(n):
        swaps[n].wait_recv()
        locals_[n].wait()

    def block_of(k, m, p, q):
        return full.at[k, m, p, :, q, core]

    def gather_copy(k, m, n, h):
        p, q = (
            (pair, lane),
            (pair, lane),
            (1 - pair, lane),
            (pair, lane),
            (1 - pair, lane),
            (pair, 1 - lane),
            (1 - pair, 1 - lane),
        )[n]
        span = full.at[k, m, p, h, q, core]
        if (k, m) == (2, 2):
            part_rows = slice(h % 2 * (rows // 2), (h % 2 + 1) * (rows // 2))
            span = full.at[k, m, p, h // 2, q, core, part_rows, :]
        to = (beyond, beside, beside, partner, partner, partner, partner)[n]
        return push(
            span, span, gather_send.at[k - 1, m, n, h], gather_recv.at[k - 1, m, n, h], to
        )

    share = pl.ds(pl.multiple_of(group * (width // 2), width // 2), width // 2)

    def first_copy(m, n):
        ref = rows_here.at[m]
        own = full.at[0, m, pair, head, lane, core]
        near = full.at[0, m, pair, 1 - head, lane, core]
        wide = full.at[0, m, 1 - pair, :, lane, core, :, share]
        src, dst, to = (
            (ref.at[1 - head, :, share], own.at[:, share], mate),
            (ref.at[head, :, share], own.at[:, share], beyond),
            (ref.at[1 - head, :, share], own.at[:, share], crossed),
            (ref.at[head], own, beside),
            (ref.at[head], own, partner),
            (near.at[:, share], near.at[:, share], beside),
            (near.at[:, share], near.at[:, share], across),
            (wide, wide, beside),
            (wide, wide, across),
            (wide, wide, corner),
            (near.at[:, share], near.at[:, share], corner),
            (near, near, partner),
            (block_of(0, m, pair, 1 - lane),) * 2 + (partner,),
            (block_of(0, m, 1 - pair, lane),) * 2 + (partner,),
            (block_of(0, m, 1 - pair, 1 - lane),) * 2 + (partner,),
        )[n]
        return push(src, dst, first_send.at[m, n], first_recv.at[m, n], to)

    def first_here(m):
        return pltpu.make_async_copy(
            rows_here.at[m, head], full.at[0, m, pair, head, lane, core], first_local.at[m]
        )

    def first_start():
        for m, ref in enumerate((first_ref, third_ref, second_ref)):
            pltpu.make_async_copy(ref, rows_here.at[m], first_local.at[m]).wait()
        for m in range(3):
            for n in (2, 1, 0, 3, 4):
                go(first_copy(m, n))
            first_here(m).start()

    def first_spread():
        for m in range(3):
            first_copy(m, 0).wait_recv()
            for n in (5, 10, 6):
                go(first_copy(m, n))
        for m in range(3):
            first_copy(m, 2).wait_recv()
            first_copy(m, 1).wait_recv()
            for n in (7, 9, 8):
                go(first_copy(m, n))
        swap(3, 6)
        for m in range(3):
            first_copy(m, 6).wait_recv()
            go(first_copy(m, 11))
            for n in (3, 5, 10):
                first_copy(m, n).wait_recv()
            go(first_copy(m, 12))
        for m in range(3):
            first_copy(m, 8).wait_recv()
            go(first_copy(m, 13))
            first_copy(m, 7).wait_recv()
            first_copy(m, 9).wait_recv()
            go(first_copy(m, 14))

    def first_end(m):
        first_here(m).wait()
        for n in (4, 11, 12, 13, 14):
            first_copy(m, n).wait_recv()

    def pieces(k, m):
        return range(4 if (k, m) == (2, 2) else 2)

    def gather_own(k, m, h):
        for n in (0, 1, 3):
            go(gather_copy(k, m, n, h))

    def gather_beyond(k, m):
        for h in pieces(k, m):
            gather_copy(k, m, 0, h).wait_recv()
            go(gather_copy(k, m, 2, h))
            go(gather_copy(k, m, 4, h))

    def gather_beside(k, m, n):
        for h in pieces(k, m):
            gather_copy(k, m, n, h).wait_recv()
            go(gather_copy(k, m, n + 4, h))

    def gather_end(k, m):
        for n in range(3, 7):
            for h in pieces(k, m):
                gather_copy(k, m, n, h).wait_recv()

    def core_copy(t):
        return push(
            core_out.at[t], core_in.at[t], sum_send.at[t], sum_recv.at[t], partner
        )

    def side_copy(t, p, n, h):
        return push(
            side_out.at[t, p, h],
            side_in.at[t, p, h],
            side_send.at[t, n, h],
            side_recv.at[t, n, h],
            beside,
        )

    def far_copy(t, h):
        return push(
            far_out.at[t, h], far_in.at[t, h], side_send.at[t, 2, h], side_recv.at[t, 2, h], beyond
        )

    def core_start(t):
        core_out[t] = part[t, :, :, :, 1 - core].astype(jnp.bfloat16)
        go(core_copy(t))

    def core_sum(t, p, q, h):
        return part[t, p, h, q, core] + core_in[t, p, h, q].astype(jnp.float32)

    def side_piece(t, n):
        if n == 0:
            core_copy(t).wait_recv()
        p = 1 - pair if n == 0 else pair
        for h in range(2):
            side_out[t, p, h] = core_sum(t, p, 1 - lane, h).astype(jnp.bfloat16)
            go(side_copy(t, p, n, h))

    def side_start(ts):
        for n in (0, 1):
            for t in ts:
                side_piece(t, n)

    def far_start(t):
        p = 1 - pair
        for h in range(2):
            side_copy(t, p, 0, h).wait_recv()
            far_out[t, h] = (
                core_sum(t, p, lane, h) + side_in[t, p, h].astype(jnp.float32)
            ).astype(jnp.bfloat16)
            go(far_copy(t, h))

    def total_of(t, h):
        side_copy(t, pair, 1, h).wait_recv()
        near = core_sum(t, pair, lane, h) + side_in[t, pair, h].astype(jnp.float32)
        far_copy(t, h).wait_recv()
        return near + far_in[t, h].astype(jnp.float32)

    order = (2, 0, 1)

    def whole(k, m):
        return full[k, m].reshape(hidden_units, width)

    def forward(k, x):
        gate = dot_nt(x, whole(k, 0))
        up = dot_nt(x, whole(k, 1))
        sig = jax.nn.sigmoid(gate)
        return gate, up, sig, (gate * sig * up).astype(jnp.bfloat16)

    def keys_forward(j):
        gate, up, sig, hidden = forward(0, keys[j])
        gates[...] = gate
        ups[...] = up
        hiddens[...] = hidden

    def steps(j):
        row = jnp.where(head == 0, rates[j, 0:1, :], rates[j, 1:2, :])
        rate = jnp.transpose(jnp.broadcast_to(row, (128, row.shape[1])))[:, 0:1]
        scaled = (rate * values[j].astype(jnp.float32)).astype(jnp.bfloat16)
        part[3 * j + 2] = dot_tn(scaled, hiddens[...]).reshape(part.shape[1:])
        core_start(3 * j + 2)
        if j == 0:
            first_end(2)
        back = dot_nn(scaled, whole(0, 2))
        gate = gates[...]
        sig = jax.nn.sigmoid(gate)
        x = keys[j]
        d_gate = (back * ups[...] * sig * (1.0 + gate * (1.0 - sig))).astype(jnp.bfloat16)
        part[3 * j] = dot_tn(d_gate, x).reshape(part.shape[1:])
        core_start(3 * j)
        d_up = (back * gate * sig).astype(jnp.bfloat16)
        part[3 * j + 1] = dot_tn(d_up, x).reshape(part.shape[1:])
        core_start(3 * j + 1)

    outs = []

    def read_hidden(k):
        gate, up, sig, hidden = forward(k, queries[k])
        hiddens[...] = hidden

    def read_out(k):
        result[k] = dot_nt(hiddens[...], whole(k, 2)).astype(jnp.bfloat16)
        send_out(k)
        keep_out(k)

    def send_out(k):
        away = push(
            result.at[k, other_slot, :],
            out_ref.at[k, :, mine],
            out_send.at[k],
            out_recv.at[k],
            mate,
        )
        away.start()
        outs.append(away)

    def keep_out(k):
        here = pltpu.make_async_copy(
            result.at[k, slot, :], out_ref.at[k, :, mine], out_local.at[k]
        )
        here.start()
        outs.append(here)

    first_start()
    swap(0, 3)
    first_spread()
    for m in range(2):
        first_end(m)
    for n in range(0, 3):
        ready(n)
    keys_forward(0)
    steps(0)
    side_start(order)
    for m in order:
        far_start(m)
    for n in range(3, 6):
        ready(n)
    keys_forward(1)
    steps(1)
    for m in order:
        side_piece(3 + m, 0)
    for m in order:
        side_piece(3 + m, 1)
    swap(6, 8)
    for m in order:
        for h in range(2):
            moment = total_of(m, h)
            step_own[m, h] = moment
            old = full[0, m, pair, h, lane, core].astype(jnp.float32)
            fresh = renorm(old, old + moment)
            weight_own[m, h] = fresh
            full[1, m, pair, h, lane, core] = fresh.astype(jnp.bfloat16)
            gather_own(1, m, h)
    decay = decay_ref[head]
    last = (0, 1, 2)
    for m in last:
        far_start(3 + m)
    for m in order:
        gather_beyond(1, m)
        gather_beside(1, m, 1)
    ready(6)
    read_hidden(0)
    read_out(0)
    for m in last:
        for h in range(2):
            moment = decay * step_own[m, h] + total_of(3 + m, h)
            old = weight_own[m, h]
            fresh = renorm(old, old + moment)
            full[2, m, pair, h, lane, core] = fresh.astype(jnp.bfloat16)
            for piece in (2 * h, 2 * h + 1) if m == 2 else (h,):
                gather_own(2, m, piece)
    swap(8, 9)
    for m in order:
        gather_beside(1, m, 2)
    for m in last:
        gather_beyond(2, m)
        gather_beside(2, m, 1)
    for m in range(3):
        gather_end(1, m)
    ready(7)
    read_hidden(1)
    read_out(1)
    ready(8)
    for m in range(2):
        gather_beside(2, m, 2)
    for m in range(2):
        gather_end(2, m)
    gate, up, sig, hidden = forward(2, queries[2])
    hiddens[...] = hidden
    for n in (3, 5):
        for h in pieces(2, 2):
            gather_copy(2, 2, n, h).wait_recv()
    columns = width // 2
    for n, p in enumerate((pair, 1 - pair)):
        if n == 1:
            gather_beside(2, 2, 2)
            for e in (4, 6):
                for h in pieces(2, 2):
                    gather_copy(2, 2, e, h).wait_recv()
        some = pl.ds(pl.multiple_of(p * columns, columns), columns)
        down = full[2, 2, p].reshape(columns, width)
        result[2, :, some] = dot_nt(hiddens[...], down).astype(jnp.bfloat16)
        place = pl.ds(pl.multiple_of(head * width + p * columns, columns), columns)
        away = push(
            result.at[2, other_slot, some],
            out_ref.at[2, :, place],
            out_send.at[2 + n],
            out_recv.at[2 + n],
            mate,
        )
        away.start()
        outs.append(away)
    keep_out(2)

    for n in range(len(pairs)):
        swaps[n].wait_send()
    for copy in sent:
        copy.wait_send()
    for copy in outs:
        copy.wait()


def fused_shards(query, key, value, rate, first, third, second, decay):
    blocks, tokens, features = query.shape
    heads, rows, width = first.shape
    hidden = 16 * rows
    span = 2 * tokens
    anywhere = pl.BlockSpec(memory_space=pl.ANY)
    dma = pltpu.SemaphoreType.DMA
    low, wide = jnp.bfloat16, jnp.float32
    return pl.pallas_call(
        kernel,
        out_shape=pltpu.VMEM(query.shape, low),
        in_specs=[anywhere] * 7 + [pl.BlockSpec(memory_space=pltpu.SMEM)],
        out_specs=pl.BlockSpec(memory_space=pltpu.VMEM),
        scratch_shapes=[
            pltpu.VMEM((3, span, width), low),
            pltpu.VMEM((2, span, width), low),
            pltpu.VMEM((2, span, width), low),
            pltpu.VMEM((2, heads, span), wide),
            pltpu.VMEM((3, 3, 2, 2, 2, 2, rows, width), low),
            pltpu.VMEM((6, 2, 2, 2, 2, rows, width), wide),
            pltpu.VMEM((6, 2, 2, 2, rows, width), low),
            pltpu.VMEM((6, 2, 2, 2, rows, width), low),
            pltpu.VMEM((6, 2, 2, rows, width), low),
            pltpu.VMEM((6, 2, 2, rows, width), low),
            pltpu.VMEM((6, 2, rows, width), low),
            pltpu.VMEM((6, 2, rows, width), low),
            pltpu.VMEM((3, 2, rows, width), wide),
            pltpu.VMEM((3, 2, rows, width), wide),
            pltpu.VMEM((3, span, width), low),
            pltpu.VMEM((span, hidden), wide),
            pltpu.VMEM((span, hidden), wide),
            pltpu.VMEM((span, hidden), low),
            dma((9,)),
            dma((9,)),
            dma((9,)),
            dma((2, 3, 7, 4)),
            dma((2, 3, 7, 4)),
            dma((3, 15)),
            dma((3, 15)),
            dma((3,)),
            pltpu.VMEM((3, heads, rows, width), low),
            dma((6,)),
            dma((6,)),
            dma((6, 3, 2)),
            dma((6, 3, 2)),
            dma((4,)),
            dma((4,)),
            dma((3,)),
        ],
        compiler_params=pltpu.CompilerParams(
            collective_id=0, has_side_effects=True, vmem_limit_bytes=60 * 1024 * 1024
        ),
    )(query, key, value, jnp.swapaxes(rate, 1, 2), first, third, second, decay)


def solution(mesh):
    placed = (
        P(None, ("groups", "tok"), None),
        P(None, ("groups", "tok"), None),
        P(None, ("groups", "tok"), None),
        P(None, ("groups", "tok"), None),
        P(None, "tok", None),
        P(None, "tok", None),
        P(None, "tok", None),
        P(),
    )
    chips = mesh.shape["tok"] // 2

    def body(*arrays):
        rows = arrays[4].shape[1]
        if rows % 16 or chips != 8 or arrays[4].shape[0] != 2 or mesh.shape["groups"] != 2:
            return shards(*arrays)
        return fused_shards(*arrays)

    return jax.shard_map(
        body,
        mesh=mesh,
        in_specs=placed,
        out_specs=P(None, ("groups", "tok"), None),
        check_vma=False,
    )
```

```python
import jax
import jax.numpy as jnp
from jax import lax
from jax.experimental import pallas as pl
from jax.experimental.pallas import tpu as pltpu
from jax.sharding import PartitionSpec as P

MESH = pl.DeviceIdType.MESH


def forward_parts(weights, inputs):
    first, third, second = weights
    length = inputs.shape[0]
    head_count = first.shape[0]
    shaped = inputs.reshape(length, head_count, -1)
    pre_gate = jnp.einsum("thd,hfd->htf", shaped, first, preferred_element_type=jnp.float32)
    pre_up = jnp.einsum("thd,hfd->htf", shaped, third, preferred_element_type=jnp.float32)
    hidden = (jax.nn.silu(pre_gate) * pre_up).astype(jnp.bfloat16)
    return (shaped, pre_gate, pre_up, hidden)


def apply_block(weights, inputs):
    shaped, pre_gate, pre_up, hidden = forward_parts(weights, inputs)
    result = jnp.einsum("htf,hdf->thd", hidden, weights[2], preferred_element_type=jnp.float32)
    return result.reshape(inputs.shape[0], -1).astype(jnp.bfloat16)


def partial_steps(weights, keys, values, rates):
    shaped, pre_gate, pre_up, hidden = forward_parts(weights, keys)
    length = keys.shape[0]
    head_count = weights[0].shape[0]
    scaled = (
        rates[:, :, None] * values.reshape(length, head_count, -1).astype(jnp.float32)
    ).astype(jnp.bfloat16)
    step_second = jnp.einsum("thd,htf->hdf", scaled, hidden, preferred_element_type=jnp.float32)
    back = jnp.einsum("thd,hdf->htf", scaled, weights[2], preferred_element_type=jnp.float32)
    sig_gate = jax.nn.sigmoid(pre_gate)
    d_gate = (back * pre_up * sig_gate * (1.0 + pre_gate * (1.0 - sig_gate))).astype(jnp.bfloat16)
    d_up = (back * pre_gate * sig_gate).astype(jnp.bfloat16)
    step_first = jnp.einsum("htf,thd->hfd", d_gate, shaped, preferred_element_type=jnp.float32)
    step_third = jnp.einsum("htf,thd->hfd", d_up, shaped, preferred_element_type=jnp.float32)
    return (step_first, step_third, step_second)


def renorm(old, moved):
    old_norm = jnp.sqrt(jnp.sum(old * old, axis=-1, keepdims=True) + 1e-06)
    moved_norm = jnp.sqrt(jnp.sum(moved * moved, axis=-1, keepdims=True) + 1e-06)
    return moved * old_norm / moved_norm


def shards(
    query_tokens,
    key_tokens,
    value_tokens,
    learn_rates,
    fast_first,
    fast_third,
    fast_second,
    momentum_decay,
):
    owned_zero = jnp.stack([fast_first, fast_third, fast_second])
    full_zero = lax.all_gather(owned_zero, "tok", axis=2, tiled=True)
    terms_zero = partial_steps(full_zero, key_tokens[0], value_tokens[0], learn_rates[0])
    terms_one = partial_steps(full_zero, key_tokens[1], value_tokens[1], learn_rates[1])
    step_zero = lax.psum_scatter(
        jnp.stack(terms_zero).astype(jnp.bfloat16), "tok", scatter_dimension=2, tiled=True
    ).astype(jnp.float32)
    step_one = lax.psum_scatter(
        jnp.stack(terms_one).astype(jnp.bfloat16), "tok", scatter_dimension=2, tiled=True
    ).astype(jnp.float32)
    out_zero = apply_block(full_zero, query_tokens[0])
    decay = momentum_decay[None, :, None, None]
    weights_zero = owned_zero.astype(jnp.float32)
    weights_one = renorm(weights_zero, weights_zero + step_zero)
    full_one = lax.all_gather(weights_one.astype(jnp.bfloat16), "tok", axis=2, tiled=True)
    weights_two = renorm(weights_one, weights_one + decay * step_zero + step_one)
    full_two = lax.all_gather(weights_two.astype(jnp.bfloat16), "tok", axis=2, tiled=True)
    out_one = apply_block(full_one, query_tokens[1])
    out_two = apply_block(full_two, query_tokens[2])
    return jnp.stack([out_zero, out_one, out_two])


def dot_nt(a, b):
    return lax.dot_general(a, b, (((1,), (1,)), ((), ())), preferred_element_type=jnp.float32)


def dot_nn(a, b):
    return lax.dot_general(a, b, (((1,), (0,)), ((), ())), preferred_element_type=jnp.float32)


def dot_tn(a, b):
    return lax.dot_general(a, b, (((0,), (0,)), ((), ())), preferred_element_type=jnp.float32)


def kernel(
    query_ref,
    key_ref,
    value_ref,
    rate_ref,
    first_ref,
    third_ref,
    second_ref,
    decay_ref,
    out_ref,
    queries,
    keys,
    values,
    rates,
    full,
    part,
    core_out,
    core_in,
    side_out,
    side_in,
    far_out,
    far_in,
    step_own,
    weight_own,
    result,
    gates,
    ups,
    hiddens,
    swap_send,
    swap_recv,
    local_sem,
    gather_send,
    gather_recv,
    first_send,
    first_recv,
    first_local,
    rows_here,
    sum_send,
    sum_recv,
    side_send,
    side_recv,
    out_send,
    out_recv,
    out_local,
):
    index = lax.axis_index("tok")
    core = index % 2
    lane = (index // 2) % 2
    head = (index // 4) % 2
    pair = index // 8
    group = lax.axis_index("groups")
    across = {"groups": 1 - group}
    partner = {"tok": index + 1 - 2 * core}
    beside = {"tok": index + 2 - 4 * lane}
    mate = {"tok": index + 4 - 8 * head}
    beyond = {"tok": index + 8 - 16 * pair}
    crossed = {"tok": index + 12 - 8 * head - 16 * pair}
    corner = {"groups": 1 - group, "tok": index + 2 - 4 * lane}
    rows = first_ref.shape[1]
    tokens = key_ref.shape[1]
    width = first_ref.shape[2]
    hidden_units = 16 * rows

    for m, ref in enumerate((first_ref, third_ref, second_ref)):
        pltpu.make_async_copy(ref, rows_here.at[m], first_local.at[m]).start()

    barrier = pltpu.get_barrier_semaphore()
    others = (crossed, beyond, corner, mate, beside, across, partner)
    for other in others:
        pl.semaphore_signal(barrier, inc=1, device_id=other, device_id_type=MESH)
    pl.semaphore_wait(barrier, len(others))

    sent = []

    def push(src, dst, send_sem, recv_sem, to):
        return pltpu.make_async_remote_copy(
            src_ref=src,
            dst_ref=dst,
            send_sem=send_sem,
            recv_sem=recv_sem,
            device_id=to,
            device_id_type=MESH,
        )

    def go(copy):
        copy.start()
        sent.append(copy)

    mine = pl.ds(pl.multiple_of(head * width, width), width)
    theirs = pl.ds(pl.multiple_of((1 - head) * width, width), width)
    slot = pl.ds(pl.multiple_of(head * tokens, tokens), tokens)
    other_slot = pl.ds(pl.multiple_of((1 - head) * tokens, tokens), tokens)

    pairs = []
    for b in range(2):
        pairs.append((key_ref.at[b, :, theirs], key_ref.at[b, :, mine], keys.at[b, slot, :]))
        pairs.append((value_ref.at[b, :, theirs], value_ref.at[b, :, mine], values.at[b, slot, :]))
        pairs.append((rate_ref.at[b], rate_ref.at[b], rates.at[b, :, slot]))
    for b in range(3):
        pairs.append((query_ref.at[b, :, theirs], query_ref.at[b, :, mine], queries.at[b, slot, :]))
    swaps = {}
    locals_ = {}

    def swap(first, last):
        for n in range(first, last):
            away, here, target = pairs[n]
            swaps[n] = push(away, target, swap_send.at[n], swap_recv.at[n], mate)
            swaps[n].start()
            locals_[n] = pltpu.make_async_copy(here, target, local_sem.at[n])
            locals_[n].start()

    def ready(n):
        swaps[n].wait_recv()
        locals_[n].wait()

    def block_of(k, m, p, q):
        return full.at[k, m, p, :, q, core]

    def gather_copy(k, m, n, h):
        p, q = (
            (pair, lane),
            (pair, lane),
            (1 - pair, lane),
            (pair, lane),
            (1 - pair, lane),
            (pair, 1 - lane),
            (1 - pair, 1 - lane),
        )[n]
        span = full.at[k, m, p, h, q, core]
        to = (beyond, beside, beside, partner, partner, partner, partner)[n]
        return push(
            span, span, gather_send.at[k - 1, m, n, h], gather_recv.at[k - 1, m, n, h], to
        )

    share = pl.ds(pl.multiple_of(group * (width // 2), width // 2), width // 2)

    def first_copy(m, n):
        ref = rows_here.at[m]
        own = full.at[0, m, pair, head, lane, core]
        near = full.at[0, m, pair, 1 - head, lane, core]
        wide = full.at[0, m, 1 - pair, :, lane, core, :, share]
        src, dst, to = (
            (ref.at[1 - head, :, share], own.at[:, share], mate),
            (ref.at[head, :, share], own.at[:, share], beyond),
            (ref.at[1 - head, :, share], own.at[:, share], crossed),
            (ref.at[head], own, beside),
            (ref.at[head], own, partner),
            (near.at[:, share], near.at[:, share], beside),
            (near.at[:, share], near.at[:, share], across),
            (wide, wide, beside),
            (wide, wide, across),
            (wide, wide, corner),
            (near.at[:, share], near.at[:, share], corner),
            (near, near, partner),
            (block_of(0, m, pair, 1 - lane),) * 2 + (partner,),
            (block_of(0, m, 1 - pair, lane),) * 2 + (partner,),
            (block_of(0, m, 1 - pair, 1 - lane),) * 2 + (partner,),
        )[n]
        return push(src, dst, first_send.at[m, n], first_recv.at[m, n], to)

    def first_here(m):
        return pltpu.make_async_copy(
            rows_here.at[m, head], full.at[0, m, pair, head, lane, core], first_local.at[m]
        )

    def first_start():
        for m, ref in enumerate((first_ref, third_ref, second_ref)):
            pltpu.make_async_copy(ref, rows_here.at[m], first_local.at[m]).wait()
        for m in range(3):
            for n in (2, 1, 0, 3, 4):
                go(first_copy(m, n))
            first_here(m).start()

    def first_spread():
        for m in range(3):
            first_copy(m, 0).wait_recv()
            for n in (5, 10, 6):
                go(first_copy(m, n))
        for m in range(3):
            first_copy(m, 2).wait_recv()
            first_copy(m, 1).wait_recv()
            for n in (7, 9, 8):
                go(first_copy(m, n))
        for m in range(3):
            first_copy(m, 6).wait_recv()
            go(first_copy(m, 11))
            for n in (3, 5, 10):
                first_copy(m, n).wait_recv()
            go(first_copy(m, 12))
        for m in range(3):
            first_copy(m, 8).wait_recv()
            go(first_copy(m, 13))
            first_copy(m, 7).wait_recv()
            first_copy(m, 9).wait_recv()
            go(first_copy(m, 14))

    def first_end(m):
        first_here(m).wait()
        for n in (4, 11, 12, 13, 14):
            first_copy(m, n).wait_recv()

    def gather_own(k, m, h):
        for n in (0, 1, 3):
            go(gather_copy(k, m, n, h))

    def gather_beyond(k, m):
        for h in range(2):
            gather_copy(k, m, 0, h).wait_recv()
            go(gather_copy(k, m, 2, h))
            go(gather_copy(k, m, 4, h))

    def gather_beside(k, m, n):
        for h in range(2):
            gather_copy(k, m, n, h).wait_recv()
            go(gather_copy(k, m, n + 4, h))

    def gather_end(k, m):
        for n in range(3, 7):
            for h in range(2):
                gather_copy(k, m, n, h).wait_recv()

    def core_copy(t):
        return push(
            core_out.at[t], core_in.at[t], sum_send.at[t], sum_recv.at[t], partner
        )

    def side_copy(t, p, n, h):
        return push(
            side_out.at[t, p, h],
            side_in.at[t, p, h],
            side_send.at[t, n, h],
            side_recv.at[t, n, h],
            beside,
        )

    def far_copy(t, h):
        return push(
            far_out.at[t, h], far_in.at[t, h], side_send.at[t, 2, h], side_recv.at[t, 2, h], beyond
        )

    def core_start(t):
        core_out[t] = part[t, :, :, :, 1 - core].astype(jnp.bfloat16)
        go(core_copy(t))

    def core_sum(t, p, q, h):
        return part[t, p, h, q, core] + core_in[t, p, h, q].astype(jnp.float32)

    def side_piece(t, n):
        if n == 0:
            core_copy(t).wait_recv()
        p = 1 - pair if n == 0 else pair
        for h in range(2):
            side_out[t, p, h] = core_sum(t, p, 1 - lane, h).astype(jnp.bfloat16)
            go(side_copy(t, p, n, h))

    def side_start(ts):
        for n in (0, 1):
            for t in ts:
                side_piece(t, n)

    def far_start(t):
        p = 1 - pair
        for h in range(2):
            side_copy(t, p, 0, h).wait_recv()
            far_out[t, h] = (
                core_sum(t, p, lane, h) + side_in[t, p, h].astype(jnp.float32)
            ).astype(jnp.bfloat16)
            go(far_copy(t, h))

    def total_of(t, h):
        side_copy(t, pair, 1, h).wait_recv()
        near = core_sum(t, pair, lane, h) + side_in[t, pair, h].astype(jnp.float32)
        far_copy(t, h).wait_recv()
        return near + far_in[t, h].astype(jnp.float32)

    order = (2, 0, 1)

    def whole(k, m):
        return full[k, m].reshape(hidden_units, width)

    def forward(k, x):
        gate = dot_nt(x, whole(k, 0))
        up = dot_nt(x, whole(k, 1))
        sig = jax.nn.sigmoid(gate)
        return gate, up, sig, (gate * sig * up).astype(jnp.bfloat16)

    def keys_forward(j):
        gate, up, sig, hidden = forward(0, keys[j])
        gates[...] = gate
        ups[...] = up
        hiddens[...] = hidden

    def steps(j):
        row = jnp.where(head == 0, rates[j, 0:1, :], rates[j, 1:2, :])
        rate = jnp.transpose(jnp.broadcast_to(row, (128, row.shape[1])))[:, 0:1]
        scaled = (rate * values[j].astype(jnp.float32)).astype(jnp.bfloat16)
        part[3 * j + 2] = dot_tn(scaled, hiddens[...]).reshape(part.shape[1:])
        core_start(3 * j + 2)
        if j == 0:
            first_end(2)
        back = dot_nn(scaled, whole(0, 2))
        gate = gates[...]
        sig = jax.nn.sigmoid(gate)
        x = keys[j]
        d_gate = (back * ups[...] * sig * (1.0 + gate * (1.0 - sig))).astype(jnp.bfloat16)
        part[3 * j] = dot_tn(d_gate, x).reshape(part.shape[1:])
        core_start(3 * j)
        d_up = (back * gate * sig).astype(jnp.bfloat16)
        part[3 * j + 1] = dot_tn(d_up, x).reshape(part.shape[1:])
        core_start(3 * j + 1)

    outs = []

    def read_hidden(k):
        gate, up, sig, hidden = forward(k, queries[k])
        hiddens[...] = hidden

    def read_out(k):
        result[k] = dot_nt(hiddens[...], whole(k, 2)).astype(jnp.bfloat16)
        send_out(k)
        keep_out(k)

    def send_out(k):
        away = push(
            result.at[k, other_slot, :],
            out_ref.at[k, :, mine],
            out_send.at[k],
            out_recv.at[k],
            mate,
        )
        away.start()
        outs.append(away)

    def keep_out(k):
        here = pltpu.make_async_copy(
            result.at[k, slot, :], out_ref.at[k, :, mine], out_local.at[k]
        )
        here.start()
        outs.append(here)

    first_start()
    swap(0, 3)
    first_spread()
    swap(3, 6)
    for m in range(2):
        first_end(m)
    for n in range(0, 3):
        ready(n)
    keys_forward(0)
    steps(0)
    side_start(order)
    for m in order:
        far_start(m)
    for n in range(3, 6):
        ready(n)
    keys_forward(1)
    steps(1)
    for m in order:
        side_piece(3 + m, 0)
    for m in order:
        side_piece(3 + m, 1)
    swap(6, 8)
    for m in order:
        for h in range(2):
            moment = total_of(m, h)
            step_own[m, h] = moment
            old = full[0, m, pair, h, lane, core].astype(jnp.float32)
            fresh = renorm(old, old + moment)
            weight_own[m, h] = fresh
            full[1, m, pair, h, lane, core] = fresh.astype(jnp.bfloat16)
            gather_own(1, m, h)
    decay = decay_ref[head]
    last = (0, 1, 2)
    for m in last:
        far_start(3 + m)
    for m in order:
        gather_beyond(1, m)
        gather_beside(1, m, 1)
    ready(6)
    read_hidden(0)
    read_out(0)
    for m in last:
        for h in range(2):
            moment = decay * step_own[m, h] + total_of(3 + m, h)
            old = weight_own[m, h]
            fresh = renorm(old, old + moment)
            full[2, m, pair, h, lane, core] = fresh.astype(jnp.bfloat16)
            gather_own(2, m, h)
    swap(8, 9)
    for m in order:
        gather_beside(1, m, 2)
    for m in last:
        gather_beyond(2, m)
        gather_beside(2, m, 1)
    for m in range(3):
        gather_end(1, m)
    ready(7)
    read_hidden(1)
    read_out(1)
    ready(8)
    for m in range(2):
        gather_beside(2, m, 2)
    for m in range(2):
        gather_end(2, m)
    gate, up, sig, hidden = forward(2, queries[2])
    hiddens[...] = hidden
    for n in (3, 5):
        for h in range(2):
            gather_copy(2, 2, n, h).wait_recv()
    columns = width // 2
    for n, p in enumerate((pair, 1 - pair)):
        if n == 1:
            gather_beside(2, 2, 2)
            for e in (4, 6):
                for h in range(2):
                    gather_copy(2, 2, e, h).wait_recv()
        some = pl.ds(pl.multiple_of(p * columns, columns), columns)
        down = full[2, 2, p].reshape(columns, width)
        result[2, :, some] = dot_nt(hiddens[...], down).astype(jnp.bfloat16)
        place = pl.ds(pl.multiple_of(head * width + p * columns, columns), columns)
        away = push(
            result.at[2, other_slot, some],
            out_ref.at[2, :, place],
            out_send.at[2 + n],
            out_recv.at[2 + n],
            mate,
        )
        away.start()
        outs.append(away)
    keep_out(2)

    for n in range(len(pairs)):
        swaps[n].wait_send()
    for copy in sent:
        copy.wait_send()
    for copy in outs:
        copy.wait()


def fused_shards(query, key, value, rate, first, third, second, decay):
    blocks, tokens, features = query.shape
    heads, rows, width = first.shape
    hidden = 16 * rows
    span = 2 * tokens
    anywhere = pl.BlockSpec(memory_space=pl.ANY)
    dma = pltpu.SemaphoreType.DMA
    low, wide = jnp.bfloat16, jnp.float32
    return pl.pallas_call(
        kernel,
        out_shape=pltpu.VMEM(query.shape, low),
        in_specs=[anywhere] * 7 + [pl.BlockSpec(memory_space=pltpu.SMEM)],
        out_specs=pl.BlockSpec(memory_space=pltpu.VMEM),
        scratch_shapes=[
            pltpu.VMEM((3, span, width), low),
            pltpu.VMEM((2, span, width), low),
            pltpu.VMEM((2, span, width), low),
            pltpu.VMEM((2, heads, span), wide),
            pltpu.VMEM((3, 3, 2, 2, 2, 2, rows, width), low),
            pltpu.VMEM((6, 2, 2, 2, 2, rows, width), wide),
            pltpu.VMEM((6, 2, 2, 2, rows, width), low),
            pltpu.VMEM((6, 2, 2, 2, rows, width), low),
            pltpu.VMEM((6, 2, 2, rows, width), low),
            pltpu.VMEM((6, 2, 2, rows, width), low),
            pltpu.VMEM((6, 2, rows, width), low),
            pltpu.VMEM((6, 2, rows, width), low),
            pltpu.VMEM((3, 2, rows, width), wide),
            pltpu.VMEM((3, 2, rows, width), wide),
            pltpu.VMEM((3, span, width), low),
            pltpu.VMEM((span, hidden), wide),
            pltpu.VMEM((span, hidden), wide),
            pltpu.VMEM((span, hidden), low),
            dma((9,)),
            dma((9,)),
            dma((9,)),
            dma((2, 3, 7, 2)),
            dma((2, 3, 7, 2)),
            dma((3, 15)),
            dma((3, 15)),
            dma((3,)),
            pltpu.VMEM((3, heads, rows, width), low),
            dma((6,)),
            dma((6,)),
            dma((6, 3, 2)),
            dma((6, 3, 2)),
            dma((4,)),
            dma((4,)),
            dma((3,)),
        ],
        compiler_params=pltpu.CompilerParams(
            collective_id=0, has_side_effects=True, vmem_limit_bytes=60 * 1024 * 1024
        ),
    )(query, key, value, jnp.swapaxes(rate, 1, 2), first, third, second, decay)


def solution(mesh):
    placed = (
        P(None, ("groups", "tok"), None),
        P(None, ("groups", "tok"), None),
        P(None, ("groups", "tok"), None),
        P(None, ("groups", "tok"), None),
        P(None, "tok", None),
        P(None, "tok", None),
        P(None, "tok", None),
        P(),
    )
    chips = mesh.shape["tok"] // 2

    def body(*arrays):
        rows = arrays[4].shape[1]
        if rows % 16 or chips != 8 or arrays[4].shape[0] != 2 or mesh.shape["groups"] != 2:
            return shards(*arrays)
        return fused_shards(*arrays)

    return jax.shard_map(
        body,
        mesh=mesh,
        in_specs=placed,
        out_specs=P(None, ("groups", "tok"), None),
        check_vma=False,
    )
```
